32 devices in a mesh: row: 4 (over x, core), col: 8 (over z, y).
Axes of the slice: x: 2, y: 2, z: 4, core: 2. Of those that a mesh axis runs over, the one named last changes fastest.
Arguments:
- rhs: float32 [32768, 512], P('col', 'row'), may hold values from -6 to 6
- factors: bfloat16 [32768, 2048], P('col', 'row'), may hold values from -0.15625 to 0.15625
- diag_inv: float32 [4, 512, 512], replicated, may hold values from -2 to 2, as said below
Outputs:
- solution: float32 [32768, 512], P('col', 'row')
The draws below stay inside these ranges and needn't reach their ends.
Inputs may be any that keep to these rules, and one draw needn't show every extreme that they name: `diag_inv`: entries off the diagonal of each block lie within 2 / sqrt(512) in magnitude; diagonal entries lie in 0.5 to 2.
All inputs are finite; a program needn't handle non-finite values.
Results may differ from the reference program's by a relative error of at most 0.0038.
Values may be sent and summed in bfloat16 or wider, within the bound.
A program may use at most 128 MiB of HBM per device.

```python
import jax
import jax.numpy as jnp
from jax import lax

NB = 512
STEPS = 4
NW = 2048
ROWS = 32768
SPAN = 8192
RHS = 512


def draw_diag_inv(key, part):
    base = jax.random.fold_in(key, 7)
    key_low, key_up, key_dia = jax.random.split(base, 3)
    scale = 0.5 / jnp.sqrt(jnp.float32(NB))
    lower_part = jnp.clip(jax.random.normal(key_low, (STEPS, NB, NB), jnp.float32), -4.0, 4.0) * scale
    upper_part = jnp.clip(jax.random.normal(key_up, (STEPS, NB, NB), jnp.float32), -4.0, 4.0) * scale
    diagonal = jnp.exp(jax.random.uniform(key_dia, (STEPS, NB), jnp.float32, jnp.log(0.5), jnp.log(2.0)))
    index = jnp.arange(NB)
    below = index[:, None] > index[None, :]
    above = index[:, None] < index[None, :]
    packed = jnp.where(below[None], lower_part, jnp.where(above[None], upper_part, 0.0))
    return (packed + diagonal[:, :, None] * jnp.eye(NB, dtype=jnp.float32)[None]).astype(jnp.float32)


def block_levels(own_key, shape, cuts, smallest, high):
    loudness = 1.0
    for dim, blocks in cuts:
        draws = jax.random.uniform(jax.random.fold_in(jax.random.fold_in(own_key, 6), dim), (blocks,), jnp.float32, smallest / len(cuts), high / len(cuts))
        loudness = loudness * jnp.repeat(jnp.exp(draws), shape[dim] // blocks).reshape((-1,) + (1,) * (len(shape) - 1 - dim))
    return loudness


def gaussian(rng, extent, scale, most, shards=(), held_as=jnp.bfloat16):
    factor_of = block_levels(rng, extent, shards, -0.22, 0.18) if shards else 1.0
    values = jax.random.normal(rng, extent, jnp.float32) * scale * factor_of
    return jnp.minimum(jnp.maximum(values, -most), most).astype(held_as)


def setup_inputs(seed: int = 0) -> dict:
    arg_keys = jax.random.split(jax.random.key(seed), 4)
    rhs = gaussian(arg_keys[0], (ROWS, RHS), 1.0, 6.0, ((0, 8), (1, 4)), jnp.float32)
    factors = gaussian(arg_keys[1], (ROWS, NW), (16 * NW // 25) ** -0.5, 0.15625, ((0, 8), (1, 4)))
    diag_inv = draw_diag_inv(jax.random.fold_in(arg_keys[3], 71), 0)
    return dict(rhs=rhs, factors=factors, diag_inv=diag_inv)


def reference(rhs, factors, diag_inv):
    index = jnp.arange(NB)
    strict_lower = index[:, None] > index[None, :]
    eye = jnp.eye(NB, dtype=jnp.float32)
    work = rhs.astype(jnp.float32)
    for step in range(STEPS):
        lower_inv = jnp.where(strict_lower, diag_inv[step], jnp.float32(0.0)) + eye
        first = step * SPAN
        solved = jnp.dot(lower_inv, work[first:first + NB], precision=lax.Precision.HIGHEST, preferred_element_type=jnp.float32)
        work = work.at[first:first + NB].set(solved)
        below = first + NB
        if below < ROWS:
            product = jnp.dot(factors[below:, step * NB:(step + 1) * NB], solved.astype(jnp.bfloat16), preferred_element_type=jnp.float32)
            work = work.at[below:].add(-product)
    for step in reversed(range(STEPS)):
        upper_inv = jnp.triu(diag_inv[step])
        first = step * SPAN
        solved = jnp.dot(upper_inv, work[first:first + NB], precision=lax.Precision.HIGHEST, preferred_element_type=jnp.float32)
        work = work.at[first:first + NB].set(solved)
        if first > 0:
            product = jnp.dot(factors[:first, step * NB:(step + 1) * NB], solved.astype(jnp.bfloat16), preferred_element_type=jnp.float32)
            work = work.at[:first].add(-product)
    return work
```

```python
import functools

import jax
import jax.numpy as jnp
from jax import lax
from jax.experimental import pallas as pl
from jax.experimental.pallas import tpu as pltpu
from jax.sharding import PartitionSpec as P

MESH = pl.DeviceIdType.MESH
F32 = jnp.float32
BF16 = jnp.bfloat16
CHUNKS = 8


def remote(src, dst, send_sem, recv_sem, **device):
    return pltpu.make_async_remote_copy(
        src_ref=src,
        dst_ref=dst,
        send_sem=send_sem,
        recv_sem=recv_sem,
        device_id=device,
        device_id_type=MESH,
    )


def dot(a, b):
    return jnp.dot(a, b, preferred_element_type=F32)


def split(value):
    high = value.astype(BF16)
    return high, (value - high.astype(F32)).astype(BF16)


def kernel(
    n_row, n_col, steps, block,
    rhs_ref, factors_ref, diag_ref, out_ref,
    diag, low_hi, low_lo, up_hi, up_lo, panel, solved, last, work, gathered,
    send1, recv1, own1, send2, recv2,
    diag_sem, f_send, f_recv, f_fwd, s_chain, s_side, s_row, s_recv, s_last, g_local, g_recv,
    one_send, one_recv, two_send, two_recv,
):
    rows_dev, width = rhs_ref.shape
    cols = factors_ref.shape[1]
    pieces = block // cols
    chips = n_row // 2
    side = n_col // steps
    row = lax.axis_index("row")
    col = lax.axis_index("col")
    chip, core = row // 2, row % 2
    sibling = chip * 2 + 1 - core
    zone, lane = col // side, col % side
    owner = lane == 0
    base = zone * side

    diag_copy = pltpu.make_async_copy(diag_ref.at[zone], diag, diag_sem)
    diag_copy.start()

    barrier = pltpu.get_barrier_semaphore()
    for d in range(1, n_row):
        pl.semaphore_signal(barrier, inc=1, device_id={"row": (row + d) % n_row}, device_id_type=MESH)
    for d in range(1, n_col):
        pl.semaphore_signal(barrier, inc=1, device_id={"col": (col + d) % n_col}, device_id_type=MESH)
    diag_copy.wait()
    pl.semaphore_wait(barrier, n_row + n_col - 2)

    window = factors_ref.at[pl.ds(0, block)]
    far = [((chip + d) % chips) * 2 + core for d in range(1, chips)]
    sends_panel = jnp.logical_and(owner, row // pieces != zone)

    def panel_copy(d):
        return remote(window, panel.at[row], f_send.at[d], f_recv.at[row], row=far[d - 1] if d else sibling)

    @pl.when(sends_panel)
    def _():
        for d in list(range(1, chips)) + [0]:
            panel_copy(d).start()

    @pl.when(owner)
    def _():
        down = lax.broadcasted_iota(jnp.int32, (block, block), 0)
        across = lax.broadcasted_iota(jnp.int32, (block, block), 1)
        matrix = diag[...]
        low_hi[...], low_lo[...] = split(jnp.where(down > across, matrix, 0.0))
        up_hi[...], up_lo[...] = split(jnp.where(down <= across, matrix, 0.0))
        work[...] = rhs_ref[pl.ds(0, block)]

    def solve(hi, lo):
        high, low = split(work[...])
        return dot(hi[...], high) + (dot(hi[...], low) + dot(lo[...], high))

    def forward_piece(source):
        return remote(panel.at[source], panel.at[source], f_fwd.at[source // 2], f_recv.at[source], row=sibling)

    def arrive_panel(j):
        for p in range(pieces):
            source = j * pieces + p

            @pl.when(source != row)
            def _():
                forward_piece(source).wait_recv()

            @pl.when(jnp.logical_and(source != row, source % 2 == core))
            def _():
                forward_piece(source).start()

            @pl.when(source == row)
            def _():
                panel[row] = factors_ref[pl.ds(0, block)]

    def chain_copy(t, j):
        target = jnp.where(t <= zone, zone + 1, zone - 1)
        return remote(solved.at[j], solved.at[j], s_chain.at[t], s_recv.at[j], col=target * side)

    def chain_sends(t):
        return jnp.where(t <= zone, zone < steps - 1, zone > 0)

    def side_copy(t, j, d):
        return remote(solved.at[j], solved.at[j], s_side.at[t, d], s_recv.at[j], col=base + d)

    def row_copy(t, j, p):
        dest = j * pieces + p
        part = solved.at[j, pl.ds(p * cols, cols)]
        return remote(
            part, gathered.at[core, :, pl.ds(pl.multiple_of(chip * width, width), width)],
            s_row.at[t, p], g_recv.at[row], row=dest,
        )

    def local_copy(j, p):
        part = solved.at[j, pl.ds(p * cols, cols)]
        return pltpu.make_async_copy(
            part, gathered.at[core, :, pl.ds(pl.multiple_of(chip * width, width), width)], g_local
        )

    for t in range(steps):
        j = jnp.where(t <= zone, t, steps + zone - t)
        mine = jnp.logical_and(owner, t == zone)

        @pl.when(jnp.logical_and(owner, t != zone))
        def _():
            arrive_panel(j)

        @pl.when(mine)
        def _():
            value = work[...] + solve(low_hi, low_lo)
            work[...] = value
            solved[j] = value.astype(BF16)

        @pl.when(jnp.logical_not(mine))
        def _():
            chain_copy(t, j).wait_recv()

        @pl.when(jnp.logical_and(owner, chain_sends(t)))
        def _():
            chain_copy(t, j).start()

        @pl.when(owner)
        def _():
            for d in range(1, side):
                side_copy(t, j, d).start()

        for p in range(pieces):
            @pl.when(j * pieces + p != row)
            def _():
                row_copy(t, j, p).start()

            @pl.when(j * pieces + p == row)
            def _():
                local_copy(j, p).start()

        @pl.when(jnp.logical_and(owner, t != zone))
        def _():
            total = work[...]
            for p in range(pieces):
                total = total - dot(panel[j * pieces + p], solved[j, pl.ds(p * cols, cols)])
            work[...] = total

    last_copy = remote(last, solved.at[zone], s_last, s_recv.at[zone], col=jnp.where(zone > 0, zone - 1, 0) * side)

    @pl.when(owner)
    def _():
        value = solve(up_hi, up_lo)
        work[...] = value
        last[...] = value.astype(BF16)

    @pl.when(jnp.logical_and(owner, zone > 0))
    def _():
        last_copy.start()

    local_copy(0, 0).wait()
    for d in range(1, n_row):
        source = (row + d) % n_row
        remote(
            gathered.at[source % 2, :, pl.ds(pl.multiple_of((source // 2) * width, width), width)],
            gathered.at[source % 2, :, pl.ds(pl.multiple_of((source // 2) * width, width), width)],
            g_local, g_recv.at[source], row=source,
        ).wait_recv()

    step_rows = rows_dev // CHUNKS

    def span(m):
        return pl.ds(pl.multiple_of(m * step_rows, step_rows), step_rows)

    def one_copy(m):
        return remote(send1.at[m], recv1.at[m], one_send.at[m], one_recv.at[m], row=sibling)

    def two_copy(m, d):
        return remote(send2.at[m, d - 1], recv2.at[m, d - 1], two_send.at[m, d - 1], two_recv.at[m, d - 1], row=far[d - 1])

    def first(m, carry):
        send1[m] = dot(factors_ref[span(m)], gathered[1 - core]).astype(BF16)
        one_copy(m).start()
        return carry

    def second(m, carry):
        own1[m] = dot(factors_ref[span(m)], gathered[core])
        one_copy(m).wait_recv()
        for d in range(1, chips):
            there = pl.ds(pl.multiple_of(((chip + d) % chips) * width, width), width)
            send2[m, d - 1] = (own1[m, :, there] + recv1[m, :, there].astype(F32)).astype(BF16)
            two_copy(m, d).start()
        return carry

    def third(m, carry):
        here = pl.ds(pl.multiple_of(chip * width, width), width)
        total = own1[m, :, here] + recv1[m, :, here].astype(F32)
        for d in range(1, chips):
            two_copy(m, d).wait_recv()
            total = total + recv2[m, d - 1].astype(F32)
        out_ref[span(m)] = rhs_ref[span(m)] - total
        return carry

    def finish(m, carry):
        one_copy(m).wait_send()
        for d in range(1, chips):
            two_copy(m, d).wait_send()
        return carry

    lax.fori_loop(0, CHUNKS, first, 0)
    lax.fori_loop(0, CHUNKS, second, 0)
    lax.fori_loop(0, CHUNKS, third, 0)

    @pl.when(owner)
    def _():
        out_ref[pl.ds(0, block)] = work[...]

    lax.fori_loop(0, CHUNKS, finish, 0)

    @pl.when(sends_panel)
    def _():
        for d in range(chips):
            panel_copy(d).wait_send()

    for t in range(steps):
        j = jnp.where(t <= zone, t, steps + zone - t)

        @pl.when(jnp.logical_and(owner, t != zone))
        def _():
            for p in range(pieces):
                source = j * pieces + p

                @pl.when(jnp.logical_and(source != row, source % 2 == core))
                def _():
                    forward_piece(source).wait_send()

        @pl.when(jnp.logical_and(owner, chain_sends(t)))
        def _():
            chain_copy(t, j).wait_send()

        @pl.when(owner)
        def _():
            for d in range(1, side):
                side_copy(t, j, d).wait_send()

        for p in range(pieces):
            @pl.when(j * pieces + p != row)
            def _():
                row_copy(t, j, p).wait_send()

    @pl.when(jnp.logical_and(owner, zone > 0))
    def _():
        last_copy.wait_send()


def body(rhs, factors, diag_inv):
    n_row, n_col = lax.axis_size("row"), lax.axis_size("col")
    rows_dev, width = rhs.shape
    cols = factors.shape[1]
    steps, block = diag_inv.shape[:2]
    pieces, chips, side = block // cols, n_row // 2, n_col // steps
    step_rows = rows_dev // CHUNKS
    dma = pltpu.SemaphoreType.DMA
    vmem = pl.BlockSpec(memory_space=pltpu.VMEM)
    return pl.pallas_call(
        functools.partial(kernel, n_row, n_col, steps, block),
        out_shape=jax.ShapeDtypeStruct(rhs.shape, F32),
        in_specs=[vmem, vmem, pl.BlockSpec(memory_space=pl.ANY)],
        out_specs=vmem,
        scratch_shapes=[
            pltpu.VMEM((block, block), F32),
            pltpu.VMEM((block, block), BF16),
            pltpu.VMEM((block, block), BF16),
            pltpu.VMEM((block, block), BF16),
            pltpu.VMEM((block, block), BF16),
            pltpu.VMEM((n_row, block, cols), BF16),
            pltpu.VMEM((steps, block, width), BF16),
            pltpu.VMEM((block, width), BF16),
            pltpu.VMEM((block, width), F32),
            pltpu.VMEM((2, cols, chips * width), BF16),
            pltpu.VMEM((CHUNKS, step_rows, chips * width), BF16),
            pltpu.VMEM((CHUNKS, step_rows, chips * width), BF16),
            pltpu.VMEM((CHUNKS, step_rows, chips * width), F32),
            pltpu.VMEM((CHUNKS, chips - 1, step_rows, width), BF16),
            pltpu.VMEM((CHUNKS, chips - 1, step_rows, width), BF16),
            dma, dma((chips,)), dma((n_row,)), dma((chips,)),
            dma((steps,)), dma((steps, side)), dma((steps, pieces)), dma((steps,)), dma, dma, dma((n_row,)),
            dma((CHUNKS,)), dma((CHUNKS,)), dma((CHUNKS, chips - 1)), dma((CHUNKS, chips - 1)),
        ],
        compiler_params=pltpu.CompilerParams(
            collective_id=0, has_side_effects=True, vmem_limit_bytes=60 * 1024 * 1024
        ),
    )(rhs, factors, diag_inv)


def solution(mesh):
    placed = (P("col", "row"), P("col", "row"), P())
    return jax.shard_map(
        body, mesh=mesh, in_specs=placed, out_specs=P("col", "row"), check_vma=False
    )
```

```python
import functools

import jax
import jax.numpy as jnp
from jax import lax
from jax.experimental import pallas as pl
from jax.experimental.pallas import tpu as pltpu
from jax.sharding import PartitionSpec as P

MESH = pl.DeviceIdType.MESH
F32 = jnp.float32
BF16 = jnp.bfloat16
CHUNKS = 8
PARTS = 4


def remote(src, dst, send_sem, recv_sem, **device):
    return pltpu.make_async_remote_copy(
        src_ref=src,
        dst_ref=dst,
        send_sem=send_sem,
        recv_sem=recv_sem,
        device_id=device,
        device_id_type=MESH,
    )


def dot(a, b):
    return jnp.dot(a, b, preferred_element_type=F32)


def split(value):
    high = value.astype(BF16)
    return high, (value - high.astype(F32)).astype(BF16)


def kernel(
    n_row, n_col, steps, block,
    rhs_ref, factors_ref, diag_ref, out_ref,
    diag, low_hi, low_lo, up_hi, up_lo, panel, solved, last, work, gathered,
    send1, recv1, own1, send2, recv2,
    diag_sem, f_send, f_recv, f_fwd, s_chain, s_side, s_row, s_recv, s_last, g_local, g_recv,
    one_send, one_recv, two_send, two_recv,
):
    rows_dev, width = rhs_ref.shape
    cols = factors_ref.shape[1]
    pieces = block // cols
    chips = n_row // 2
    side = n_col // steps
    row = lax.axis_index("row")
    col = lax.axis_index("col")
    chip, core = row // 2, row % 2
    sibling = chip * 2 + 1 - core
    zone, lane = col // side, col % side
    owner = lane == 0
    base = zone * side

    diag_copy = pltpu.make_async_copy(diag_ref.at[zone], diag, diag_sem)
    diag_copy.start()

    barrier = pltpu.get_barrier_semaphore()
    for d in range(1, n_row):
        pl.semaphore_signal(barrier, inc=1, device_id={"row": (row + d) % n_row}, device_id_type=MESH)
    for d in range(1, n_col):
        pl.semaphore_signal(barrier, inc=1, device_id={"col": (col + d) % n_col}, device_id_type=MESH)
    diag_copy.wait()
    pl.semaphore_wait(barrier, n_row + n_col - 2)

    window = factors_ref.at[pl.ds(0, block)]
    far = [((chip + d) % chips) * 2 + core for d in range(1, chips)]
    sends_panel = jnp.logical_and(owner, row // pieces != zone)

    def panel_copy(d):
        return remote(window, panel.at[row], f_send.at[d], f_recv.at[row], row=far[d - 1] if d else sibling)

    @pl.when(sends_panel)
    def _():
        for d in list(range(1, chips)) + [0]:
            panel_copy(d).start()

    @pl.when(owner)
    def _():
        down = lax.broadcasted_iota(jnp.int32, (block, block), 0)
        across = lax.broadcasted_iota(jnp.int32, (block, block), 1)
        matrix = diag[...]
        low_hi[...], low_lo[...] = split(jnp.where(down > across, matrix, 0.0))
        up_hi[...], up_lo[...] = split(jnp.where(down <= across, matrix, 0.0))
        work[...] = rhs_ref[pl.ds(0, block)]

    part_rows = block // PARTS

    def part(q):
        return pl.ds(q * part_rows, part_rows)

    def solve(hi, lo, high, low, q):
        return dot(hi[part(q)], high) + (dot(hi[part(q)], low) + dot(lo[part(q)], high))

    def forward_piece(source):
        return remote(panel.at[source], panel.at[source], f_fwd.at[source // 2], f_recv.at[source], row=sibling)

    def arrive_panel(j):
        for p in range(pieces):
            source = j * pieces + p

            @pl.when(source != row)
            def _():
                forward_piece(source).wait_recv()

            @pl.when(jnp.logical_and(source != row, source % 2 == core))
            def _():
                forward_piece(source).start()

            @pl.when(source == row)
            def _():
                panel[row] = factors_ref[pl.ds(0, block)]

    def chain_copy(t, j, q):
        target = jnp.where(t <= zone, zone + 1, zone - 1)
        piece = solved.at[j, part(q)]
        return remote(piece, piece, s_chain.at[t, q], s_recv.at[j, q], col=target * side)

    def chain_sends(t):
        return jnp.where(t <= zone, zone < steps - 1, zone > 0)

    def side_copy(t, j, d, q):
        piece = solved.at[j, part(q)]
        return remote(piece, piece, s_side.at[t, d, q], s_recv.at[j, q], col=base + d)

    def pass_on(t, j, q):
        @pl.when(jnp.logical_and(owner, chain_sends(t)))
        def _():
            chain_copy(t, j, q).start()

        @pl.when(owner)
        def _():
            for d in range(1, side):
                side_copy(t, j, d, q).start()

    def update(j, q):
        first_row = (q - 1) * part_rows
        total = work[...]
        depth = min(2 * part_rows, cols)
        for start in range(first_row, first_row + 2 * part_rows, depth):
            total = total - dot(
                panel[j * pieces + start // cols, :, pl.ds(start % cols, depth)],
                solved[j, pl.ds(start, depth)],
            )
        work[...] = total

    def row_copy(t, j, p):
        dest = j * pieces + p
        part = solved.at[j, pl.ds(p * cols, cols)]
        return remote(
            part, gathered.at[core, :, pl.ds(pl.multiple_of(chip * width, width), width)],
            s_row.at[t, p], g_recv.at[row], row=dest,
        )

    def local_copy(j, p):
        part = solved.at[j, pl.ds(p * cols, cols)]
        return pltpu.make_async_copy(
            part, gathered.at[core, :, pl.ds(pl.multiple_of(chip * width, width), width)], g_local
        )

    step_rows = rows_dev // CHUNKS

    def span(m):
        return pl.ds(pl.multiple_of(m * step_rows, step_rows), step_rows)

    def one_copy(m):
        return remote(send1.at[m], recv1.at[m], one_send.at[m], one_recv.at[m], row=sibling)

    def two_copy(m, d):
        return remote(send2.at[m, d - 1], recv2.at[m, d - 1], two_send.at[m, d - 1], two_recv.at[m, d - 1], row=far[d - 1])

    def first(m, carry):
        send1[m] = dot(factors_ref[span(m)], gathered[1 - core]).astype(BF16)
        one_copy(m).start()
        return carry

    def second(m, carry):
        own1[m] = dot(factors_ref[span(m)], gathered[core])
        one_copy(m).wait_recv()
        for d in range(1, chips):
            there = pl.ds(pl.multiple_of(((chip + d) % chips) * width, width), width)
            send2[m, d - 1] = (own1[m, :, there] + recv1[m, :, there].astype(F32)).astype(BF16)
            two_copy(m, d).start()
        return carry

    def third(m, carry):
        here = pl.ds(pl.multiple_of(chip * width, width), width)
        total = own1[m, :, here] + recv1[m, :, here].astype(F32)
        for d in range(1, chips):
            two_copy(m, d).wait_recv()
            total = total + recv2[m, d - 1].astype(F32)
        out_ref[span(m)] = rhs_ref[span(m)] - total
        return carry

    def finish(m, carry):
        one_copy(m).wait_send()
        for d in range(1, chips):
            two_copy(m, d).wait_send()
        return carry

    mine_block = row // pieces
    place = jnp.where(mine_block <= zone, mine_block, steps + zone - mine_block)
    early = jnp.logical_and(place < steps - 1, lane > 0)

    def first_products():
        local_copy(0, 0).wait()
        for d in range(1, n_row):
            source = (row + d) % n_row
            piece = gathered.at[source % 2, :, pl.ds(pl.multiple_of((source // 2) * width, width), width)]
            remote(piece, piece, g_local, g_recv.at[source], row=source).wait_recv()
        lax.fori_loop(0, CHUNKS, first, 0)

    for t in range(steps):
        j = jnp.where(t <= zone, t, steps + zone - t)
        mine = jnp.logical_and(owner, t == zone)
        if t == steps - 1:
            pl.when(early)(first_products)

        @pl.when(jnp.logical_and(owner, t != zone))
        def _():
            arrive_panel(j)

        @pl.when(mine)
        def _():
            high, low = split(work[...])
            for q in range(PARTS):
                value = work[part(q)] + solve(low_hi, low_lo, high, low, q)
                work[part(q)] = value
                solved[j, part(q)] = value.astype(BF16)
                pass_on(t, j, q)

        @pl.when(jnp.logical_not(mine))
        def _():
            for q in range(PARTS):
                chain_copy(t, j, q).wait_recv()
                pass_on(t, j, q)
                if q % 2:
                    @pl.when(owner)
                    def _():
                        update(j, q)

        for p in range(pieces):
            @pl.when(j * pieces + p != row)
            def _():
                row_copy(t, j, p).start()

            @pl.when(j * pieces + p == row)
            def _():
                local_copy(j, p).start()

    def last_copy(q):
        target = jnp.where(zone > 0, zone - 1, 0) * side
        return remote(last.at[part(q)], solved.at[zone, part(q)], s_last.at[q], s_recv.at[zone, q], col=target)

    @pl.when(owner)
    def _():
        high, low = split(work[...])
        for q in range(PARTS):
            value = solve(up_hi, up_lo, high, low, q)
            work[part(q)] = value
            last[part(q)] = value.astype(BF16)

            @pl.when(zone > 0)
            def _():
                last_copy(q).start()

    pl.when(jnp.logical_not(early))(first_products)
    lax.fori_loop(0, CHUNKS, second, 0)
    lax.fori_loop(0, CHUNKS, third, 0)

    @pl.when(owner)
    def _():
        out_ref[pl.ds(0, block)] = work[...]

    lax.fori_loop(0, CHUNKS, finish, 0)

    @pl.when(sends_panel)
    def _():
        for d in range(chips):
            panel_copy(d).wait_send()

    for t in range(steps):
        j = jnp.where(t <= zone, t, steps + zone - t)

        @pl.when(jnp.logical_and(owner, t != zone))
        def _():
            for p in range(pieces):
                source = j * pieces + p

                @pl.when(jnp.logical_and(source != row, source % 2 == core))
                def _():
                    forward_piece(source).wait_send()

        @pl.when(jnp.logical_and(owner, chain_sends(t)))
        def _():
            for q in range(PARTS):
                chain_copy(t, j, q).wait_send()

        @pl.when(owner)
        def _():
            for d in range(1, side):
                for q in range(PARTS):
                    side_copy(t, j, d, q).wait_send()

        for p in range(pieces):
            @pl.when(j * pieces + p != row)
            def _():
                row_copy(t, j, p).wait_send()

    @pl.when(jnp.logical_and(owner, zone > 0))
    def _():
        for q in range(PARTS):
            last_copy(q).wait_send()


def body(rhs, factors, diag_inv):
    n_row, n_col = lax.axis_size("row"), lax.axis_size("col")
    rows_dev, width = rhs.shape
    cols = factors.shape[1]
    steps, block = diag_inv.shape[:2]
    pieces, chips, side = block // cols, n_row // 2, n_col // steps
    step_rows = rows_dev // CHUNKS
    dma = pltpu.SemaphoreType.DMA
    vmem = pl.BlockSpec(memory_space=pltpu.VMEM)
    return pl.pallas_call(
        functools.partial(kernel, n_row, n_col, steps, block),
        out_shape=jax.ShapeDtypeStruct(rhs.shape, F32),
        in_specs=[vmem, vmem, pl.BlockSpec(memory_space=pl.ANY)],
        out_specs=vmem,
        scratch_shapes=[
            pltpu.VMEM((block, block), F32),
            pltpu.VMEM((block, block), BF16),
            pltpu.VMEM((block, block), BF16),
            pltpu.VMEM((block, block), BF16),
            pltpu.VMEM((block, block), BF16),
            pltpu.VMEM((n_row, block, cols), BF16),
            pltpu.VMEM((steps, block, width), BF16),
            pltpu.VMEM((block, width), BF16),
            pltpu.VMEM((block, width), F32),
            pltpu.VMEM((2, cols, chips * width), BF16),
            pltpu.VMEM((CHUNKS, step_rows, chips * width), BF16),
            pltpu.VMEM((CHUNKS, step_rows, chips * width), BF16),
            pltpu.VMEM((CHUNKS, step_rows, chips * width), F32),
            pltpu.VMEM((CHUNKS, chips - 1, step_rows, width), BF16),
            pltpu.VMEM((CHUNKS, chips - 1, step_rows, width), BF16),
            dma, dma((chips,)), dma((n_row,)), dma((chips,)),
            dma((steps, PARTS)), dma((steps, side, PARTS)), dma((steps, pieces)), dma((steps, PARTS)), dma((PARTS,)), dma, dma((n_row,)),
            dma((CHUNKS,)), dma((CHUNKS,)), dma((CHUNKS, chips - 1)), dma((CHUNKS, chips - 1)),
        ],
        compiler_params=pltpu.CompilerParams(
            collective_id=0, has_side_effects=True, vmem_limit_bytes=60 * 1024 * 1024
        ),
    )(rhs, factors, diag_inv)


def solution(mesh):
    placed = (P("col", "row"), P("col", "row"), P())
    return jax.shard_map(
        body, mesh=mesh, in_specs=placed, out_specs=P("col", "row"), check_vma=False
    )
```

```python
import functools

import jax
import jax.numpy as jnp
from jax import lax
from jax.experimental import pallas as pl
from jax.experimental.pallas import tpu as pltpu
from jax.sharding import PartitionSpec as P

MESH = pl.DeviceIdType.MESH
F32 = jnp.float32
BF16 = jnp.bfloat16
CHUNKS = 8
PARTS = 4
GATHER = 3


def remote(src, dst, send_sem, recv_sem, **device):
    return pltpu.make_async_remote_copy(
        src_ref=src,
        dst_ref=dst,
        send_sem=send_sem,
        recv_sem=recv_sem,
        device_id=device,
        device_id_type=MESH,
    )


def dot(a, b):
    return jnp.dot(a, b, preferred_element_type=F32)


def split(value):
    high = value.astype(BF16)
    return high, (value - high.astype(F32)).astype(BF16)


def kernel(
    n_row, n_col, steps, block,
    rhs_hbm, factors_hbm, diag_ref, out_ref,
    rhs_ref, factors_ref, extra,
    diag, low_hi, low_lo, up_hi, up_lo, panel, solved, last, work, gathered,
    send1, recv1, own1, send2, recv2,
    diag_sem, f_send, f_recv, f_fwd, s_chain, s_side, s_row, s_recv, s_last, g_local, g_recv,
    one_send, one_recv, two_send, two_recv, x_send, x_recv, x_fwd, load_sem,
):
    rows_dev, width = rhs_ref.shape
    cols = factors_ref.shape[1]
    pieces = block // cols
    chips = n_row // 2
    side = n_col // steps
    row = lax.axis_index("row")
    col = lax.axis_index("col")
    chip, core = row // 2, row % 2
    sibling = chip * 2 + 1 - core
    zone, lane = col // side, col % side
    owner = lane == 0
    base = zone * side

    diag_copy = pltpu.make_async_copy(diag_ref.at[zone], diag, diag_sem)
    rhs_copy = pltpu.make_async_copy(rhs_hbm, rhs_ref, load_sem.at[0])
    factors_copy = pltpu.make_async_copy(factors_hbm, factors_ref, load_sem.at[1])
    work_copy = pltpu.make_async_copy(rhs_hbm.at[pl.ds(0, block)], work, load_sem.at[2])
    panel_own = pltpu.make_async_copy(factors_hbm.at[pl.ds(0, block)], panel.at[row], load_sem.at[3])
    diag_copy.start()
    work_copy.start()
    panel_own.start()
    factors_copy.start()
    rhs_copy.start()

    barrier = pltpu.get_barrier_semaphore()
    for d in range(1, n_row):
        pl.semaphore_signal(barrier, inc=1, device_id={"row": (row + d) % n_row}, device_id_type=MESH)
    for d in range(1, n_col):
        pl.semaphore_signal(barrier, inc=1, device_id={"col": (col + d) % n_col}, device_id_type=MESH)
    pl.semaphore_wait(barrier, n_row + n_col - 2)

    window = factors_hbm.at[pl.ds(0, block)]
    far = [((chip + d) % chips) * 2 + core for d in range(1, chips)]
    sends_panel = jnp.logical_and(owner, row // pieces != zone)

    def panel_copy(d):
        return remote(window, panel.at[row], f_send.at[d], f_recv.at[row], row=far[d - 1] if d else sibling)

    @pl.when(sends_panel)
    def _():
        for d in list(range(1, chips)) + [0]:
            panel_copy(d).start()

    step_rows = rows_dev // CHUNKS
    n_extra = jnp.maximum(GATHER - zone - jnp.where(owner, 1, 0), 0)

    def span(m):
        return pl.ds(pl.multiple_of(m * step_rows, step_rows), step_rows)

    def extra_copy(g, d):
        return remote(
            factors_hbm.at[span(CHUNKS - 1 - g)], extra.at[g, row], x_send.at[g, d], x_recv.at[g, row],
            row=far[d - 1] if d else sibling,
        )

    def extra_forward(g, source):
        return remote(extra.at[g, source], extra.at[g, source], x_fwd.at[g, source // 2], x_recv.at[g, source], row=sibling)

    def extra_start(g, carry):
        for d in range(chips):
            extra_copy(g, d).start()
        return carry

    lax.fori_loop(0, n_extra, extra_start, 0)
    diag_copy.wait()
    work_copy.wait()
    panel_own.wait()

    @pl.when(owner)
    def _():
        down = lax.broadcasted_iota(jnp.int32, (block, block), 0)
        across = lax.broadcasted_iota(jnp.int32, (block, block), 1)
        matrix = diag[...]
        low_hi[...], low_lo[...] = split(jnp.where(down > across, matrix, 0.0))
        up_hi[...], up_lo[...] = split(jnp.where(down <= across, matrix, 0.0))

    part_rows = block // PARTS

    def part(q):
        return pl.ds(q * part_rows, part_rows)

    def solve(hi, lo, high, low, q):
        return dot(hi[part(q)], high) + (dot(hi[part(q)], low) + dot(lo[part(q)], high))

    def forward_piece(source):
        return remote(panel.at[source], panel.at[source], f_fwd.at[source // 2], f_recv.at[source], row=sibling)

    def slot(t):
        return jnp.where(t <= zone, t, steps + zone - t)

    def hand_on(t):
        if t == steps:
            return
        for p in range(pieces):
            source = slot(t) * pieces + p
            here = jnp.logical_and(owner, t != zone)

            @pl.when(here & (source != row) & (source % 2 == core))
            def _():
                forward_piece(source).wait_recv()
                forward_piece(source).start()

    def arrive_panel(j):
        for p in range(pieces):
            source = j * pieces + p

            @pl.when(source % 2 != core)
            def _():
                forward_piece(source).wait_recv()

    def chain_copy(t, j, q):
        target = jnp.where(t <= zone, zone + 1, zone - 1)
        piece = solved.at[j, part(q)]
        return remote(piece, piece, s_chain.at[t, q], s_recv.at[j, q], col=target * side)

    def chain_sends(t):
        return jnp.where(t <= zone, zone < steps - 1, zone > 0)

    def side_copy(t, j, d, q):
        piece = solved.at[j, part(q)]
        return remote(piece, piece, s_side.at[t, d, q], s_recv.at[j, q], col=base + d)

    def pass_on(t, j, q):
        @pl.when(jnp.logical_and(owner, chain_sends(t)))
        def _():
            chain_copy(t, j, q).start()

        @pl.when(owner)
        def _():
            for d in range(1, side):
                side_copy(t, j, d, q).start()

    def update(j, q):
        first_row = (q - 1) * part_rows
        total = work[...]
        depth = min(2 * part_rows, cols)
        for start in range(first_row, first_row + 2 * part_rows, depth):
            total = total - dot(
                panel[j * pieces + start // cols, :, pl.ds(start % cols, depth)],
                solved[j, pl.ds(start, depth)],
            )
        work[...] = total

    def row_copy(t, j, p):
        dest = j * pieces + p
        part = solved.at[j, pl.ds(p * cols, cols)]
        return remote(
            part, gathered.at[core, :, pl.ds(pl.multiple_of(chip * width, width), width)],
            s_row.at[t, p], g_recv.at[row], row=dest,
        )

    def local_copy(j, p):
        part = solved.at[j, pl.ds(p * cols, cols)]
        return pltpu.make_async_copy(
            part, gathered.at[core, :, pl.ds(pl.multiple_of(chip * width, width), width)], g_local
        )

    def one_copy(m):
        return remote(send1.at[m], recv1.at[m], one_send.at[m], one_recv.at[m], row=sibling)

    def two_copy(m, d):
        return remote(send2.at[m, d - 1], recv2.at[m, d - 1], two_send.at[m, d - 1], two_recv.at[m, d - 1], row=far[d - 1])

    def first(m, carry):
        send1[m] = dot(factors_ref[span(m)], gathered[1 - core]).astype(BF16)
        one_copy(m).start()
        return carry

    def second(m, carry):
        own1[m] = dot(factors_ref[span(m)], gathered[core])
        one_copy(m).wait_recv()
        for d in range(1, chips):
            there = pl.ds(pl.multiple_of(((chip + d) % chips) * width, width), width)
            send2[m, d - 1] = (own1[m, :, there] + recv1[m, :, there].astype(F32)).astype(BF16)
            two_copy(m, d).start()
        return carry

    def third(m, carry):
        here = pl.ds(pl.multiple_of(chip * width, width), width)
        total = own1[m, :, here] + recv1[m, :, here].astype(F32)
        for d in range(1, chips):
            two_copy(m, d).wait_recv()
            total = total + recv2[m, d - 1].astype(F32)
        out_ref[span(m)] = rhs_ref[span(m)] - total
        return carry

    def finish(m, carry):
        one_copy(m).wait_send()
        for d in range(1, chips):
            two_copy(m, d).wait_send()
        return carry

    n_swap = CHUNKS - n_extra

    def extra_hand_on(g, carry):
        for d in range(1, chips):
            extra_forward(g, far[d - 1]).wait_recv()
            extra_forward(g, far[d - 1]).start()
        return carry

    def extra_product(g, carry):
        rows = span(CHUNKS - 1 - g)
        total = rhs_ref[rows]
        for d in range(n_row):
            source = (row + d) % n_row
            part_of = solved[source // pieces, pl.ds(pl.multiple_of((source % pieces) * cols, cols), cols)]
            if d == 0:
                total = total - dot(factors_ref[rows], part_of)
            else:
                @pl.when(source % 2 != core)
                def _():
                    extra_forward(g, source).wait_recv()

                total = total - dot(extra[g, source], part_of)
        out_ref[rows] = total
        return carry

    def extra_finish(g, carry):
        for d in range(chips):
            extra_copy(g, d).wait_send()
        for d in range(1, chips):
            extra_forward(g, far[d - 1]).wait_send()
        return carry

    def first_products():
        factors_copy.wait()
        rhs_copy.wait()
        local_copy(0, 0).wait()
        for d in range(1, n_row):
            source = (row + d) % n_row
            piece = gathered.at[source % 2, :, pl.ds(pl.multiple_of((source // 2) * width, width), width)]
            remote(piece, piece, g_local, g_recv.at[source], row=source).wait_recv()
        lax.fori_loop(0, n_swap, first, 0)

    for t in range(steps):
        j = slot(t)
        mine = jnp.logical_and(owner, t == zone)
        if t == 0:
            hand_on(t)

        @pl.when(jnp.logical_and(owner, t != zone))
        def _():
            arrive_panel(j)

        @pl.when(mine)
        def _():
            high, low = split(work[...])
            for q in range(PARTS):
                value = work[part(q)] + solve(low_hi, low_lo, high, low, q)
                work[part(q)] = value
                solved[j, part(q)] = value.astype(BF16)
                pass_on(t, j, q)

        @pl.when(jnp.logical_not(mine))
        def _():
            for q in range(PARTS):
                chain_copy(t, j, q).wait_recv()
                pass_on(t, j, q)
                if q % 2:
                    @pl.when(owner)
                    def _():
                        update(j, q)

        for p in range(pieces):
            @pl.when(j * pieces + p != row)
            def _():
                row_copy(t, j, p).start()

            @pl.when(j * pieces + p == row)
            def _():
                local_copy(j, p).start()

        hand_on(t + 1)

    def last_copy(q):
        target = jnp.where(zone > 0, zone - 1, 0) * side
        return remote(last.at[part(q)], solved.at[zone, part(q)], s_last.at[q], s_recv.at[zone, q], col=target)

    @pl.when(owner)
    def _():
        high, low = split(work[...])
        for q in range(PARTS):
            value = solve(up_hi, up_lo, high, low, q)
            work[part(q)] = value
            last[part(q)] = value.astype(BF16)

            @pl.when(zone > 0)
            def _():
                last_copy(q).start()

    first_products()
    lax.fori_loop(0, n_swap, second, 0)
    lax.fori_loop(0, n_extra, extra_hand_on, 0)
    lax.fori_loop(0, n_extra, extra_product, 0)
    lax.fori_loop(0, n_swap, third, 0)

    @pl.when(owner)
    def _():
        out_ref[pl.ds(0, block)] = work[...]

    lax.fori_loop(0, n_swap, finish, 0)
    lax.fori_loop(0, n_extra, extra_finish, 0)

    @pl.when(sends_panel)
    def _():
        for d in range(chips):
            panel_copy(d).wait_send()

    for t in range(steps):
        j = slot(t)

        @pl.when(jnp.logical_and(owner, t != zone))
        def _():
            for p in range(pieces):
                source = j * pieces + p

                @pl.when(jnp.logical_and(source != row, source % 2 == core))
                def _():
                    forward_piece(source).wait_send()

        @pl.when(jnp.logical_and(owner, chain_sends(t)))
        def _():
            for q in range(PARTS):
                chain_copy(t, j, q).wait_send()

        @pl.when(owner)
        def _():
            for d in range(1, side):
                for q in range(PARTS):
                    side_copy(t, j, d, q).wait_send()

        for p in range(pieces):
            @pl.when(j * pieces + p != row)
            def _():
                row_copy(t, j, p).wait_send()

    @pl.when(jnp.logical_and(owner, zone > 0))
    def _():
        for q in range(PARTS):
            last_copy(q).wait_send()


def body(rhs, factors, diag_inv):
    n_row, n_col = lax.axis_size("row"), lax.axis_size("col")
    rows_dev, width = rhs.shape
    cols = factors.shape[1]
    steps, block = diag_inv.shape[:2]
    pieces, chips, side = block // cols, n_row // 2, n_col // steps
    step_rows = rows_dev // CHUNKS
    dma = pltpu.SemaphoreType.DMA
    vmem = pl.BlockSpec(memory_space=pltpu.VMEM)
    return pl.pallas_call(
        functools.partial(kernel, n_row, n_col, steps, block),
        out_shape=jax.ShapeDtypeStruct(rhs.shape, F32),
        in_specs=[pl.BlockSpec(memory_space=pl.ANY)] * 3,
        out_specs=vmem,
        scratch_shapes=[
            pltpu.VMEM(rhs.shape, F32),
            pltpu.VMEM(factors.shape, BF16),
            pltpu.VMEM((GATHER, n_row, step_rows, cols), BF16),
            pltpu.VMEM((block, block), F32),
            pltpu.VMEM((block, block), BF16),
            pltpu.VMEM((block, block), BF16),
            pltpu.VMEM((block, block), BF16),
            pltpu.VMEM((block, block), BF16),
            pltpu.VMEM((n_row, block, cols), BF16),
            pltpu.VMEM((steps, block, width), BF16),
            pltpu.VMEM((block, width), BF16),
            pltpu.VMEM((block, width), F32),
            pltpu.VMEM((2, cols, chips * width), BF16),
            pltpu.VMEM((CHUNKS, step_rows, chips * width), BF16),
            pltpu.VMEM((CHUNKS, step_rows, chips * width), BF16),
            pltpu.VMEM((CHUNKS, step_rows, chips * width), F32),
            pltpu.VMEM((CHUNKS, chips - 1, step_rows, width), BF16),
            pltpu.VMEM((CHUNKS, chips - 1, step_rows, width), BF16),
            dma, dma((chips,)), dma((n_row,)), dma((chips,)),
            dma((steps, PARTS)), dma((steps, side, PARTS)), dma((steps, pieces)), dma((steps, PARTS)), dma((PARTS,)), dma, dma((n_row,)),
            dma((CHUNKS,)), dma((CHUNKS,)), dma((CHUNKS, chips - 1)), dma((CHUNKS, chips - 1)),
            dma((GATHER, chips)), dma((GATHER, n_row)), dma((GATHER, chips)), dma((4,)),
        ],
        compiler_params=pltpu.CompilerParams(
            collective_id=0, has_side_effects=True, vmem_limit_bytes=60 * 1024 * 1024
        ),
    )(rhs, factors, diag_inv)


def solution(mesh):
    placed = (P("col", "row"), P("col", "row"), P())
    return jax.shard_map(
        body, mesh=mesh, in_specs=placed, out_specs=P("col", "row"), check_vma=False
    )
```

```python
import functools

import jax
import jax.numpy as jnp
from jax import lax
from jax.experimental import pallas as pl
from jax.experimental.pallas import tpu as pltpu
from jax.sharding import PartitionSpec as P

MESH = pl.DeviceIdType.MESH
F32 = jnp.float32
BF16 = jnp.bfloat16
CHUNKS = 8
PARTS = 4
GATHER = 3


def remote(src, dst, send_sem, recv_sem, **device):
    return pltpu.make_async_remote_copy(
        src_ref=src,
        dst_ref=dst,
        send_sem=send_sem,
        recv_sem=recv_sem,
        device_id=device,
        device_id_type=MESH,
    )


def dot(a, b):
    return jnp.dot(a, b, preferred_element_type=F32)


def split(value):
    high = value.astype(BF16)
    return high, (value - high.astype(F32)).astype(BF16)


def kernel(
    n_row, n_col, steps, block,
    rhs_hbm, factors_hbm, diag_ref, out_ref,
    rhs_ref, factors_ref, extra,
    diag, low_hi, low_lo, up_hi, up_lo, panel, solved, last, work, gathered,
    send1, recv1, own1, send2, recv2,
    diag_sem, f_send, f_recv, f_fwd, s_chain, s_side, s_row, s_recv, s_last, g_local, g_recv,
    one_send, one_recv, two_send, two_recv, x_send, x_recv, x_fwd, load_sem,
):
    rows_dev, width = rhs_hbm.shape
    cols = factors_ref.shape[1]
    pieces = block // cols
    chips = n_row // 2
    side = n_col // steps
    row = lax.axis_index("row")
    col = lax.axis_index("col")
    chip, core = row // 2, row % 2
    sibling = chip * 2 + 1 - core
    zone, lane = col // side, col % side
    owner = lane == 0
    base = zone * side

    diag_copy = pltpu.make_async_copy(diag_ref.at[zone], diag, diag_sem)
    rhs_copy = pltpu.make_async_copy(rhs_hbm.at[pl.ds(0, block)], rhs_ref, load_sem.at[0])
    factors_copy = pltpu.make_async_copy(factors_hbm, factors_ref, load_sem.at[1])
    work_copy = pltpu.make_async_copy(rhs_hbm.at[pl.ds(0, block)], work, load_sem.at[2])
    panel_own = pltpu.make_async_copy(factors_hbm.at[pl.ds(0, block)], panel.at[row], load_sem.at[3])
    diag_copy.start()
    work_copy.start()
    panel_own.start()
    factors_copy.start()
    rhs_copy.start()

    barrier = pltpu.get_barrier_semaphore()
    for d in range(1, n_row):
        pl.semaphore_signal(barrier, inc=1, device_id={"row": (row + d) % n_row}, device_id_type=MESH)
    for d in range(1, n_col):
        pl.semaphore_signal(barrier, inc=1, device_id={"col": (col + d) % n_col}, device_id_type=MESH)
    pl.semaphore_wait(barrier, n_row + n_col - 2)

    window = factors_hbm.at[pl.ds(0, block)]
    far = [((chip + d) % chips) * 2 + core for d in range(1, chips)]
    sends_panel = jnp.logical_and(owner, row // pieces != zone)

    def panel_copy(d):
        return remote(window, panel.at[row], f_send.at[d], f_recv.at[row], row=far[d - 1] if d else sibling)

    @pl.when(sends_panel)
    def _():
        for d in list(range(1, chips)) + [0]:
            panel_copy(d).start()

    step_rows = rows_dev // CHUNKS
    n_extra = jnp.maximum(GATHER - (zone + 1) // 2 - jnp.where(owner, 1, 0), 0)

    def span(m):
        return pl.ds(pl.multiple_of(m * step_rows, step_rows), step_rows)

    def extra_copy(g, d):
        return remote(
            factors_hbm.at[span(CHUNKS - 1 - g)], extra.at[g, row], x_send.at[g, d], x_recv.at[g, row],
            row=far[d - 1] if d else sibling,
        )

    def extra_forward(g, source):
        return remote(extra.at[g, source], extra.at[g, source], x_fwd.at[g, source // 2], x_recv.at[g, source], row=sibling)

    def extra_start(g, carry):
        for d in range(chips):
            extra_copy(g, d).start()
        return carry

    lax.fori_loop(0, n_extra, extra_start, 0)
    diag_copy.wait()
    work_copy.wait()
    panel_own.wait()

    @pl.when(owner)
    def _():
        down = lax.broadcasted_iota(jnp.int32, (block, block), 0)
        across = lax.broadcasted_iota(jnp.int32, (block, block), 1)
        matrix = diag[...]
        low_hi[...], low_lo[...] = split(jnp.where(down > across, matrix, 0.0))
        up_hi[...], up_lo[...] = split(jnp.where(down <= across, matrix, 0.0))

    part_rows = block // PARTS

    def part(q):
        return pl.ds(q * part_rows, part_rows)

    def solve(hi, lo, high, low, q):
        return dot(hi[part(q)], high) + (dot(hi[part(q)], low) + dot(lo[part(q)], high))

    def forward_piece(source):
        return remote(panel.at[source], panel.at[source], f_fwd.at[source // 2], f_recv.at[source], row=sibling)

    def slot(t):
        return jnp.where(t <= zone, t, steps + zone - t)

    def hand_on(t):
        if t == steps:
            return
        for p in range(pieces):
            source = slot(t) * pieces + p
            here = jnp.logical_and(owner, t != zone)

            @pl.when(here & (source != row) & (source % 2 == core))
            def _():
                forward_piece(source).wait_recv()
                forward_piece(source).start()

    def arrive_panel(j):
        for p in range(pieces):
            source = j * pieces + p

            @pl.when(source % 2 != core)
            def _():
                forward_piece(source).wait_recv()

    def chain_copy(t, j, q):
        target = jnp.where(t <= zone, zone + 1, zone - 1)
        piece = solved.at[j, part(q)]
        return remote(piece, piece, s_chain.at[t, q], s_recv.at[j, q], col=target * side)

    def chain_sends(t):
        return jnp.where(t <= zone, zone < steps - 1, zone > 0)

    def side_copy(t, j, d, q):
        piece = solved.at[j, part(q)]
        return remote(piece, piece, s_side.at[t, d, q], s_recv.at[j, q], col=base + d)

    def pass_on(t, j, q):
        @pl.when(jnp.logical_and(owner, chain_sends(t)))
        def _():
            chain_copy(t, j, q).start()

        @pl.when(owner)
        def _():
            for d in range(1, side):
                side_copy(t, j, d, q).start()

    def update(j, q):
        first_row = (q - 1) * part_rows
        total = work[...]
        depth = min(2 * part_rows, cols)
        for start in range(first_row, first_row + 2 * part_rows, depth):
            total = total - dot(
                panel[j * pieces + start // cols, :, pl.ds(start % cols, depth)],
                solved[j, pl.ds(start, depth)],
            )
        work[...] = total

    per = PARTS // pieces
    my_columns = pl.ds(pl.multiple_of(chip * width, width), width)

    def row_copy(t, j, q):
        return remote(
            solved.at[j, part(q)], gathered.at[core, part(q % per), my_columns],
            s_row.at[t, q], g_recv.at[row, q % per], row=j * pieces + q // per,
        )

    def local_copy(j, q):
        return pltpu.make_async_copy(
            solved.at[j, part(q)], gathered.at[core, part(q % per), my_columns], g_local.at[q % per]
        )

    def share(t, j, q):
        @pl.when(j * pieces + q // per != row)
        def _():
            row_copy(t, j, q).start()

        @pl.when(j * pieces + q // per == row)
        def _():
            local_copy(j, q).start()

    def one_copy(m):
        return remote(send1.at[m], recv1.at[m], one_send.at[m], one_recv.at[m], row=sibling)

    def two_copy(m, d):
        return remote(send2.at[m, d - 1], recv2.at[m, d - 1], two_send.at[m, d - 1], two_recv.at[m, d - 1], row=far[d - 1])

    def first(m, carry):
        send1[m] = dot(factors_ref[span(m)], gathered[1 - core]).astype(BF16)
        one_copy(m).start()
        return carry

    def second(m, carry):
        @pl.when(m + 2 < n_swap)
        def _():
            first(m + 2, 0)

        own1[m] = dot(factors_ref[span(m)], gathered[core])
        one_copy(m).wait_recv()
        for d in range(1, chips):
            there = pl.ds(pl.multiple_of(((chip + d) % chips) * width, width), width)
            send2[m, d - 1] = (own1[m, :, there] + recv1[m, :, there].astype(F32)).astype(BF16)
            two_copy(m, d).start()
        return carry

    def third(m, carry):
        here = pl.ds(pl.multiple_of(chip * width, width), width)
        total = own1[m, :, here] + recv1[m, :, here].astype(F32)
        for d in range(1, chips):
            two_copy(m, d).wait_recv()
            total = total + recv2[m, d - 1].astype(F32)
        out_ref[span(m)] = total
        return carry

    def finish(m, carry):
        one_copy(m).wait_send()
        for d in range(1, chips):
            two_copy(m, d).wait_send()
        return carry

    n_swap = CHUNKS - n_extra

    def extra_hand_on(g, carry):
        for d in range(1, chips):
            extra_forward(g, far[d - 1]).wait_recv()
            extra_forward(g, far[d - 1]).start()
        return carry

    def extra_product(g, carry):
        rows = span(CHUNKS - 1 - g)
        total = jnp.zeros((step_rows, width), F32)
        for d in range(n_row):
            source = (row + d) % n_row
            part_of = solved[source // pieces, pl.ds(pl.multiple_of((source % pieces) * cols, cols), cols)]
            if d == 0:
                total = total + dot(factors_ref[rows], part_of)
            else:
                @pl.when(source % 2 != core)
                def _():
                    extra_forward(g, source).wait_recv()

                total = total + dot(extra[g, source], part_of)
        out_ref[rows] = total
        return carry

    def extra_finish(g, carry):
        for d in range(chips):
            extra_copy(g, d).wait_send()
        for d in range(1, chips):
            extra_forward(g, far[d - 1]).wait_send()
        return carry

    def first_products():
        factors_copy.wait()
        rhs_copy.wait()
        for q in range(per):
            local_copy(0, q).wait()
        for d in range(1, n_row):
            source = (row + d) % n_row
            for q in range(per):
                piece = gathered.at[source % 2, part(q), pl.ds(pl.multiple_of((source // 2) * width, width), width)]
                remote(piece, piece, g_local.at[q], g_recv.at[source, q], row=source).wait_recv()
        first(0, 0)
        first(1, 0)

    for t in range(steps):
        j = slot(t)
        mine = jnp.logical_and(owner, t == zone)
        if t == 0:
            hand_on(t)

        @pl.when(jnp.logical_and(owner, t != zone))
        def _():
            arrive_panel(j)

        @pl.when(mine)
        def _():
            high, low = split(work[...])
            for q in range(PARTS):
                value = work[part(q)] + solve(low_hi, low_lo, high, low, q)
                work[part(q)] = value
                solved[j, part(q)] = value.astype(BF16)
                pass_on(t, j, q)
                share(t, j, q)

        @pl.when(jnp.logical_not(mine))
        def _():
            for q in range(PARTS):
                chain_copy(t, j, q).wait_recv()
                pass_on(t, j, q)
                share(t, j, q)
                if q % 2:
                    @pl.when(owner)
                    def _():
                        update(j, q)

        hand_on(t + 1)

    def last_copy(q):
        target = jnp.where(zone > 0, zone - 1, 0) * side
        return remote(last.at[part(q)], solved.at[zone, part(q)], s_last.at[q], s_recv.at[zone, q], col=target)

    @pl.when(owner)
    def _():
        high, low = split(work[...])
        for q in range(PARTS):
            value = solve(up_hi, up_lo, high, low, q)
            work[part(q)] = value
            last[part(q)] = value.astype(BF16)

            @pl.when(zone > 0)
            def _():
                last_copy(q).start()

    first_products()
    lax.fori_loop(0, n_swap, second, 0)
    lax.fori_loop(0, n_extra, extra_hand_on, 0)
    lax.fori_loop(0, n_extra, extra_product, 0)
    lax.fori_loop(0, n_swap, third, 0)

    @pl.when(owner)
    def _():
        out_ref[pl.ds(0, block)] = rhs_ref[...] - work[...]

    lax.fori_loop(0, n_swap, finish, 0)
    lax.fori_loop(0, n_extra, extra_finish, 0)

    @pl.when(sends_panel)
    def _():
        for d in range(chips):
            panel_copy(d).wait_send()

    for t in range(steps):
        j = slot(t)

        @pl.when(jnp.logical_and(owner, t != zone))
        def _():
            for p in range(pieces):
                source = j * pieces + p

                @pl.when(jnp.logical_and(source != row, source % 2 == core))
                def _():
                    forward_piece(source).wait_send()

        @pl.when(jnp.logical_and(owner, chain_sends(t)))
        def _():
            for q in range(PARTS):
                chain_copy(t, j, q).wait_send()

        @pl.when(owner)
        def _():
            for d in range(1, side):
                for q in range(PARTS):
                    side_copy(t, j, d, q).wait_send()

        for q in range(PARTS):
            @pl.when(j * pieces + q // per != row)
            def _():
                row_copy(t, j, q).wait_send()

    @pl.when(jnp.logical_and(owner, zone > 0))
    def _():
        for q in range(PARTS):
            last_copy(q).wait_send()


def body(rhs, factors, diag_inv):
    n_row, n_col = lax.axis_size("row"), lax.axis_size("col")
    rows_dev, width = rhs.shape
    cols = factors.shape[1]
    steps, block = diag_inv.shape[:2]
    pieces, chips, side = block // cols, n_row // 2, n_col // steps
    step_rows = rows_dev // CHUNKS
    dma = pltpu.SemaphoreType.DMA
    vmem = pl.BlockSpec(memory_space=pltpu.VMEM)
    taken = pl.pallas_call(
        functools.partial(kernel, n_row, n_col, steps, block),
        out_shape=jax.ShapeDtypeStruct(rhs.shape, F32),
        in_specs=[pl.BlockSpec(memory_space=pl.ANY)] * 3,
        out_specs=vmem,
        scratch_shapes=[
            pltpu.VMEM((block, width), F32),
            pltpu.VMEM(factors.shape, BF16),
            pltpu.VMEM((GATHER, n_row, step_rows, cols), BF16),
            pltpu.VMEM((block, block), F32),
            pltpu.VMEM((block, block), BF16),
            pltpu.VMEM((block, block), BF16),
            pltpu.VMEM((block, block), BF16),
            pltpu.VMEM((block, block), BF16),
            pltpu.VMEM((n_row, block, cols), BF16),
            pltpu.VMEM((steps, block, width), BF16),
            pltpu.VMEM((block, width), BF16),
            pltpu.VMEM((block, width), F32),
            pltpu.VMEM((2, cols, chips * width), BF16),
            pltpu.VMEM((CHUNKS, step_rows, chips * width), BF16),
            pltpu.VMEM((CHUNKS, step_rows, chips * width), BF16),
            pltpu.VMEM((CHUNKS, step_rows, chips * width), F32),
            pltpu.VMEM((CHUNKS, chips - 1, step_rows, width), BF16),
            pltpu.VMEM((CHUNKS, chips - 1, step_rows, width), BF16),
            dma, dma((chips,)), dma((n_row,)), dma((chips,)),
            dma((steps, PARTS)), dma((steps, side, PARTS)), dma((steps, PARTS)), dma((steps, PARTS)), dma((PARTS,)),
            dma((PARTS // pieces,)), dma((n_row, PARTS // pieces)),
            dma((CHUNKS,)), dma((CHUNKS,)), dma((CHUNKS, chips - 1)), dma((CHUNKS, chips - 1)),
            dma((GATHER, chips)), dma((GATHER, n_row)), dma((GATHER, chips)), dma((4,)),
        ],
        compiler_params=pltpu.CompilerParams(
            collective_id=0, has_side_effects=True, vmem_limit_bytes=60 * 1024 * 1024
        ),
    )(rhs, factors, diag_inv)
    return rhs - taken


def solution(mesh):
    placed = (P("col", "row"), P("col", "row"), P())
    return jax.shard_map(
        body, mesh=mesh, in_specs=placed, out_specs=P("col", "row"), check_vma=False
    )
```

```python
import functools

import jax
import jax.numpy as jnp
from jax import lax
from jax.experimental import pallas as pl
from jax.experimental.pallas import tpu as pltpu
from jax.sharding import PartitionSpec as P

MESH = pl.DeviceIdType.MESH
F32 = jnp.float32
BF16 = jnp.bfloat16
CHUNKS = 8
PARTS = 4
GATHER = 3


def remote(src, dst, send_sem, recv_sem, **device):
    return pltpu.make_async_remote_copy(
        src_ref=src,
        dst_ref=dst,
        send_sem=send_sem,
        recv_sem=recv_sem,
        device_id=device,
        device_id_type=MESH,
    )


def dot(a, b):
    return jnp.dot(a, b, preferred_element_type=F32)


def split(value):
    high = value.astype(BF16)
    return high, (value - high.astype(F32)).astype(BF16)


def kernel(
    n_row, n_col, steps, block,
    rhs_hbm, factors_hbm, diag_ref, out_ref,
    rhs_ref, factors_ref, extra,
    diag, low_hi, low_lo, up_hi, up_lo, panel, solved, last, work, gathered,
    send1, recv1, own1, send2, recv2,
    diag_sem, f_send, f_recv, f_fwd, s_chain, s_side, s_row, s_recv, s_last, g_local, g_recv,
    one_send, one_recv, two_send, two_recv, x_send, x_recv, x_fwd, load_sem,
):
    rows_dev, width = rhs_hbm.shape
    cols = factors_ref.shape[1]
    pieces = block // cols
    chips = n_row // 2
    side = n_col // steps
    row = lax.axis_index("row")
    col = lax.axis_index("col")
    chip, core = row // 2, row % 2
    sibling = chip * 2 + 1 - core
    zone, lane = col // side, col % side
    owner = lane == 0
    base = zone * side

    diag_copy = pltpu.make_async_copy(diag_ref.at[zone], diag, diag_sem)
    rhs_copy = pltpu.make_async_copy(rhs_hbm.at[pl.ds(0, block)], rhs_ref, load_sem.at[0])
    factors_copy = pltpu.make_async_copy(factors_hbm, factors_ref, load_sem.at[1])
    work_copy = pltpu.make_async_copy(rhs_hbm.at[pl.ds(0, block)], work, load_sem.at[2])
    panel_own = pltpu.make_async_copy(factors_hbm.at[pl.ds(0, block)], panel.at[row], load_sem.at[3])
    diag_copy.start()
    work_copy.start()
    panel_own.start()
    factors_copy.start()
    rhs_copy.start()

    barrier = pltpu.get_barrier_semaphore()
    for d in range(1, n_row):
        pl.semaphore_signal(barrier, inc=1, device_id={"row": (row + d) % n_row}, device_id_type=MESH)
    for d in range(1, n_col):
        pl.semaphore_signal(barrier, inc=1, device_id={"col": (col + d) % n_col}, device_id_type=MESH)
    pl.semaphore_wait(barrier, n_row + n_col - 2)

    window = factors_hbm.at[pl.ds(0, block)]
    far = [((chip + d) % chips) * 2 + core for d in range(1, chips)]
    sends_panel = jnp.logical_and(owner, row // pieces != zone)

    def panel_copy(d):
        return remote(window, panel.at[row], f_send.at[d], f_recv.at[row], row=far[d - 1] if d else sibling)

    @pl.when(sends_panel)
    def _():
        for d in list(range(1, chips)) + [0]:
            panel_copy(d).start()

    step_rows = rows_dev // CHUNKS
    n_extra = jnp.maximum(GATHER - (zone + 1) // 2 - jnp.where(owner, 1, 0), 0)

    def span(m):
        return pl.ds(pl.multiple_of(m * step_rows, step_rows), step_rows)

    def extra_copy(g, d):
        return remote(
            factors_hbm.at[span(CHUNKS - 1 - g)], extra.at[g, row], x_send.at[g, d], x_recv.at[g, row],
            row=far[d - 1] if d else sibling,
        )

    def extra_forward(g, source):
        return remote(extra.at[g, source], extra.at[g, source], x_fwd.at[g, source // 2], x_recv.at[g, source], row=sibling)

    def extra_start(g, carry):
        for d in range(chips):
            extra_copy(g, d).start()
        return carry

    waits = jnp.logical_and(owner, zone > 0)
    lax.fori_loop(0, jnp.where(waits, 0, n_extra), extra_start, 0)
    diag_copy.wait()
    work_copy.wait()
    panel_own.wait()

    @pl.when(owner)
    def _():
        down = lax.broadcasted_iota(jnp.int32, (block, block), 0)
        across = lax.broadcasted_iota(jnp.int32, (block, block), 1)
        matrix = diag[...]
        low_hi[...], low_lo[...] = split(jnp.where(down > across, matrix, 0.0))
        up_hi[...], up_lo[...] = split(jnp.where(down <= across, matrix, 0.0))

    part_rows = block // PARTS

    def part(q):
        return pl.ds(q * part_rows, part_rows)

    def solve(hi, lo, high, low, q):
        return dot(hi[part(q)], high) + (dot(hi[part(q)], low) + dot(lo[part(q)], high))

    def forward_piece(source):
        return remote(panel.at[source], panel.at[source], f_fwd.at[source // 2], f_recv.at[source], row=sibling)

    def slot(t):
        return jnp.where(t <= zone, t, steps + zone - t)

    def hand_on(t):
        if t == steps:
            return
        for p in range(pieces):
            source = slot(t) * pieces + p
            here = jnp.logical_and(owner, t != zone)

            @pl.when(here & (source != row) & (source % 2 == core))
            def _():
                forward_piece(source).wait_recv()
                forward_piece(source).start()

    def arrive_panel(j):
        for p in range(pieces):
            source = j * pieces + p

            @pl.when(source % 2 != core)
            def _():
                forward_piece(source).wait_recv()

    def chain_copy(t, j, q):
        target = jnp.where(t <= zone, zone + 1, zone - 1)
        piece = solved.at[j, part(q)]
        return remote(piece, piece, s_chain.at[t, q], s_recv.at[j, q], col=target * side)

    def chain_sends(t):
        return jnp.where(t <= zone, zone < steps - 1, zone > 0)

    def side_copy(t, j, d, q):
        piece = solved.at[j, part(q)]
        return remote(piece, piece, s_side.at[t, d, q], s_recv.at[j, q], col=base + d)

    def pass_on(t, j, q):
        @pl.when(jnp.logical_and(owner, chain_sends(t)))
        def _():
            chain_copy(t, j, q).start()

        @pl.when(owner)
        def _():
            for d in range(1, side):
                side_copy(t, j, d, q).start()

    def update(j, q):
        first_row = (q - 1) * part_rows
        total = work[...]
        depth = min(2 * part_rows, cols)
        for start in range(first_row, first_row + 2 * part_rows, depth):
            total = total - dot(
                panel[j * pieces + start // cols, :, pl.ds(start % cols, depth)],
                solved[j, pl.ds(start, depth)],
            )
        work[...] = total

    per = PARTS // pieces
    my_columns = pl.ds(pl.multiple_of(chip * width, width), width)

    def row_copy(t, j, q):
        return remote(
            solved.at[j, part(q)], gathered.at[core, part(q % per), my_columns],
            s_row.at[t, q], g_recv.at[row, q % per], row=j * pieces + q // per,
        )

    def local_copy(j, q):
        return pltpu.make_async_copy(
            solved.at[j, part(q)], gathered.at[core, part(q % per), my_columns], g_local.at[q % per]
        )

    def share(t, j, q):
        @pl.when(j * pieces + q // per != row)
        def _():
            row_copy(t, j, q).start()

        @pl.when(j * pieces + q // per == row)
        def _():
            local_copy(j, q).start()

    def one_copy(m):
        return remote(send1.at[m], recv1.at[m], one_send.at[m], one_recv.at[m], row=sibling)

    def two_copy(m, d):
        return remote(send2.at[m, d - 1], recv2.at[m, d - 1], two_send.at[m, d - 1], two_recv.at[m, d - 1], row=far[d - 1])

    def first(m, carry):
        send1[m] = dot(factors_ref[span(m)], gathered[1 - core]).astype(BF16)
        one_copy(m).start()
        return carry

    def second(m, carry):
        @pl.when(m + 2 < n_swap)
        def _():
            first(m + 2, 0)

        own1[m] = dot(factors_ref[span(m)], gathered[core])
        one_copy(m).wait_recv()
        for d in range(1, chips):
            there = pl.ds(pl.multiple_of(((chip + d) % chips) * width, width), width)
            send2[m, d - 1] = (own1[m, :, there] + recv1[m, :, there].astype(F32)).astype(BF16)
            two_copy(m, d).start()
        return carry

    def third(m, carry):
        here = pl.ds(pl.multiple_of(chip * width, width), width)
        total = own1[m, :, here] + recv1[m, :, here].astype(F32)
        for d in range(1, chips):
            two_copy(m, d).wait_recv()
            total = total + recv2[m, d - 1].astype(F32)
        out_ref[span(m)] = total
        return carry

    def finish(m, carry):
        one_copy(m).wait_send()
        for d in range(1, chips):
            two_copy(m, d).wait_send()
        return carry

    n_swap = CHUNKS - n_extra

    def extra_hand_on(g, carry):
        for d in range(1, chips):
            extra_forward(g, far[d - 1]).wait_recv()
            extra_forward(g, far[d - 1]).start()
        return carry

    def extra_product(g, carry):
        rows = span(CHUNKS - 1 - g)
        total = jnp.zeros((step_rows, width), F32)
        for d in range(n_row):
            source = (row + d) % n_row
            part_of = solved[source // pieces, pl.ds(pl.multiple_of((source % pieces) * cols, cols), cols)]
            if d == 0:
                total = total + dot(factors_ref[rows], part_of)
            else:
                @pl.when(source % 2 != core)
                def _():
                    extra_forward(g, source).wait_recv()

                total = total + dot(extra[g, source], part_of)
        out_ref[rows] = total
        return carry

    def extra_finish(g, carry):
        for d in range(chips):
            extra_copy(g, d).wait_send()
        for d in range(1, chips):
            extra_forward(g, far[d - 1]).wait_send()
        return carry

    def first_products():
        factors_copy.wait()
        rhs_copy.wait()
        for q in range(per):
            local_copy(0, q).wait()
        for d in range(1, n_row):
            source = (row + d) % n_row
            for q in range(per):
                piece = gathered.at[source % 2, part(q), pl.ds(pl.multiple_of((source // 2) * width, width), width)]
                remote(piece, piece, g_local.at[q], g_recv.at[source, q], row=source).wait_recv()
        first(0, 0)
        first(1, 0)

    for t in range(steps):
        j = slot(t)
        mine = jnp.logical_and(owner, t == zone)
        if t == 0:
            hand_on(t)

        @pl.when(jnp.logical_and(owner, t != zone))
        def _():
            arrive_panel(j)

        @pl.when(mine)
        def _():
            high, low = split(work[...])
            for q in range(PARTS):
                value = work[part(q)] + solve(low_hi, low_lo, high, low, q)
                work[part(q)] = value
                solved[j, part(q)] = value.astype(BF16)
                pass_on(t, j, q)
                share(t, j, q)

        @pl.when(jnp.logical_not(mine))
        def _():
            for q in range(PARTS):
                chain_copy(t, j, q).wait_recv()
                pass_on(t, j, q)
                share(t, j, q)
                if q % 2:
                    @pl.when(owner)
                    def _():
                        update(j, q)

        hand_on(t + 1)
        if t == 0:
            lax.fori_loop(0, jnp.where(waits, n_extra, 0), extra_start, 0)

    def last_copy(q):
        target = jnp.where(zone > 0, zone - 1, 0) * side
        return remote(last.at[part(q)], solved.at[zone, part(q)], s_last.at[q], s_recv.at[zone, q], col=target)

    @pl.when(owner)
    def _():
        high, low = split(work[...])
        for q in range(PARTS):
            value = solve(up_hi, up_lo, high, low, q)
            work[part(q)] = value
            last[part(q)] = value.astype(BF16)

            @pl.when(zone > 0)
            def _():
                last_copy(q).start()

    first_products()
    lax.fori_loop(0, n_swap, second, 0)
    lax.fori_loop(0, n_extra, extra_hand_on, 0)
    lax.fori_loop(0, n_extra, extra_product, 0)
    lax.fori_loop(0, n_swap, third, 0)

    @pl.when(owner)
    def _():
        out_ref[pl.ds(0, block)] = rhs_ref[...] - work[...]

    lax.fori_loop(0, n_swap, finish, 0)
    lax.fori_loop(0, n_extra, extra_finish, 0)

    @pl.when(sends_panel)
    def _():
        for d in range(chips):
            panel_copy(d).wait_send()

    for t in range(steps):
        j = slot(t)

        @pl.when(jnp.logical_and(owner, t != zone))
        def _():
            for p in range(pieces):
                source = j * pieces + p

                @pl.when(jnp.logical_and(source != row, source % 2 == core))
                def _():
                    forward_piece(source).wait_send()

        @pl.when(jnp.logical_and(owner, chain_sends(t)))
        def _():
            for q in range(PARTS):
                chain_copy(t, j, q).wait_send()

        @pl.when(owner)
        def _():
            for d in range(1, side):
                for q in range(PARTS):
                    side_copy(t, j, d, q).wait_send()

        for q in range(PARTS):
            @pl.when(j * pieces + q // per != row)
            def _():
                row_copy(t, j, q).wait_send()

    @pl.when(jnp.logical_and(owner, zone > 0))
    def _():
        for q in range(PARTS):
            last_copy(q).wait_send()


def body(rhs, factors, diag_inv):
    n_row, n_col = lax.axis_size("row"), lax.axis_size("col")
    rows_dev, width = rhs.shape
    cols = factors.shape[1]
    steps, block = diag_inv.shape[:2]
    pieces, chips, side = block // cols, n_row // 2, n_col // steps
    step_rows = rows_dev // CHUNKS
    dma = pltpu.SemaphoreType.DMA
    vmem = pl.BlockSpec(memory_space=pltpu.VMEM)
    taken = pl.pallas_call(
        functools.partial(kernel, n_row, n_col, steps, block),
        out_shape=jax.ShapeDtypeStruct(rhs.shape, F32),
        in_specs=[pl.BlockSpec(memory_space=pl.ANY)] * 3,
        out_specs=vmem,
        scratch_shapes=[
            pltpu.VMEM((block, width), F32),
            pltpu.VMEM(factors.shape, BF16),
            pltpu.VMEM((GATHER, n_row, step_rows, cols), BF16),
            pltpu.VMEM((block, block), F32),
            pltpu.VMEM((block, block), BF16),
            pltpu.VMEM((block, block), BF16),
            pltpu.VMEM((block, block), BF16),
            pltpu.VMEM((block, block), BF16),
            pltpu.VMEM((n_row, block, cols), BF16),
            pltpu.VMEM((steps, block, width), BF16),
            pltpu.VMEM((block, width), BF16),
            pltpu.VMEM((block, width), F32),
            pltpu.VMEM((2, cols, chips * width), BF16),
            pltpu.VMEM((CHUNKS, step_rows, chips * width), BF16),
            pltpu.VMEM((CHUNKS, step_rows, chips * width), BF16),
            pltpu.VMEM((CHUNKS, step_rows, chips * width), F32),
            pltpu.VMEM((CHUNKS, chips - 1, step_rows, width), BF16),
            pltpu.VMEM((CHUNKS, chips - 1, step_rows, width), BF16),
            dma, dma((chips,)), dma((n_row,)), dma((chips,)),
            dma((steps, PARTS)), dma((steps, side, PARTS)), dma((steps, PARTS)), dma((steps, PARTS)), dma((PARTS,)),
            dma((PARTS // pieces,)), dma((n_row, PARTS // pieces)),
            dma((CHUNKS,)), dma((CHUNKS,)), dma((CHUNKS, chips - 1)), dma((CHUNKS, chips - 1)),
            dma((GATHER, chips)), dma((GATHER, n_row)), dma((GATHER, chips)), dma((4,)),
        ],
        compiler_params=pltpu.CompilerParams(
            collective_id=0, has_side_effects=True, vmem_limit_bytes=60 * 1024 * 1024
        ),
    )(rhs, factors, diag_inv)
    return rhs - taken


def solution(mesh):
    placed = (P("col", "row"), P("col", "row"), P())
    return jax.shard_map(
        body, mesh=mesh, in_specs=placed, out_specs=P("col", "row"), check_vma=False
    )
```

```python
import functools

import jax
import jax.numpy as jnp
from jax import lax
from jax.experimental import pallas as pl
from jax.experimental.pallas import tpu as pltpu
from jax.sharding import PartitionSpec as P

MESH = pl.DeviceIdType.MESH
F32 = jnp.float32
BF16 = jnp.bfloat16
CHUNKS = 8
PARTS = 4
GATHER = 3


def remote(src, dst, send_sem, recv_sem, **device):
    return pltpu.make_async_remote_copy(
        src_ref=src,
        dst_ref=dst,
        send_sem=send_sem,
        recv_sem=recv_sem,
        device_id=device,
        device_id_type=MESH,
    )


def dot(a, b):
    return jnp.dot(a, b, preferred_element_type=F32)


def split(value):
    high = value.astype(BF16)
    return high, (value - high.astype(F32)).astype(BF16)


def kernel(
    n_row, n_col, steps, block,
    rhs_hbm, factors_hbm, diag_ref, out_ref,
    rhs_ref, factors_ref, extra,
    diag, low_hi, low_lo, up_hi, up_lo, panel, solved, last, work, gathered,
    send1, recv1, own1, send2, recv2,
    diag_sem, f_send, f_recv, f_fwd, s_chain, s_side, s_row, s_recv, s_last, g_local, g_recv,
    one_send, one_recv, two_send, two_recv, x_send, x_recv, x_fwd, load_sem,
):
    rows_dev, width = rhs_hbm.shape
    cols = factors_ref.shape[1]
    pieces = block // cols
    chips = n_row // 2
    side = n_col // steps
    row = lax.axis_index("row")
    col = lax.axis_index("col")
    chip, core = row // 2, row % 2
    sibling = chip * 2 + 1 - core
    zone, lane = col // side, col % side
    owner = lane == 0
    base = zone * side

    diag_copy = pltpu.make_async_copy(diag_ref.at[zone], diag, diag_sem)
    rhs_copy = pltpu.make_async_copy(rhs_hbm.at[pl.ds(0, block)], rhs_ref, load_sem.at[0])
    factors_copy = pltpu.make_async_copy(factors_hbm, factors_ref, load_sem.at[1])
    work_copy = pltpu.make_async_copy(rhs_hbm.at[pl.ds(0, block)], work, load_sem.at[2])
    panel_own = pltpu.make_async_copy(factors_hbm.at[pl.ds(0, block)], panel.at[row], load_sem.at[3])
    diag_copy.start()
    work_copy.start()
    panel_own.start()
    factors_copy.start()
    rhs_copy.start()

    barrier = pltpu.get_barrier_semaphore()
    for d in range(1, n_row):
        pl.semaphore_signal(barrier, inc=1, device_id={"row": (row + d) % n_row}, device_id_type=MESH)
    for d in range(1, n_col):
        pl.semaphore_signal(barrier, inc=1, device_id={"col": (col + d) % n_col}, device_id_type=MESH)
    pl.semaphore_wait(barrier, n_row + n_col - 2)

    window = factors_hbm.at[pl.ds(0, block)]
    far = [((chip + d) % chips) * 2 + core for d in range(1, chips)]
    sends_panel = jnp.logical_and(owner, row // pieces != zone)

    def panel_copy(d):
        return remote(window, panel.at[row], f_send.at[d], f_recv.at[row], row=far[d - 1] if d else sibling)

    @pl.when(sends_panel)
    def _():
        for d in list(range(1, chips)) + [0]:
            panel_copy(d).start()

    step_rows = rows_dev // CHUNKS
    n_extra = jnp.maximum(GATHER - (zone + 1) // 2 - jnp.where(owner, 1, 0), 0)

    def span(m):
        return pl.ds(pl.multiple_of(m * step_rows, step_rows), step_rows)

    def extra_copy(g, d):
        return remote(
            factors_hbm.at[span(CHUNKS - 1 - g)], extra.at[g, row], x_send.at[g, d], x_recv.at[g, row],
            row=far[d - 1] if d else sibling,
        )

    def extra_forward(g, source):
        return remote(extra.at[g, source], extra.at[g, source], x_fwd.at[g, source // 2], x_recv.at[g, source], row=sibling)

    def extra_start(g, carry):
        for d in range(chips):
            extra_copy(g, d).start()
        return carry

    waits = jnp.logical_and(owner, zone > 0)
    lax.fori_loop(0, jnp.where(waits, 0, n_extra), extra_start, 0)
    diag_copy.wait()
    work_copy.wait()
    panel_own.wait()

    @pl.when(owner)
    def _():
        down = lax.broadcasted_iota(jnp.int32, (block, block), 0)
        across = lax.broadcasted_iota(jnp.int32, (block, block), 1)
        matrix = diag[...]
        low_hi[...], low_lo[...] = split(jnp.where(down > across, matrix, 0.0))
        up_hi[...], up_lo[...] = split(jnp.where(down <= across, matrix, 0.0))

    part_rows = block // PARTS

    def part(q):
        return pl.ds(q * part_rows, part_rows)

    def solve(hi, lo, high, low, q):
        return dot(hi[part(q)], high) + (dot(hi[part(q)], low) + dot(lo[part(q)], high))

    def forward_piece(source):
        return remote(panel.at[source], panel.at[source], f_fwd.at[source // 2], f_recv.at[source], row=sibling)

    def slot(t):
        return jnp.where(t <= zone, t, steps + zone - t)

    def hand_on(t):
        if t == steps:
            return
        for p in range(pieces):
            source = slot(t) * pieces + p
            here = jnp.logical_and(owner, t != zone)

            @pl.when(here & (source != row) & (source % 2 == core))
            def _():
                forward_piece(source).wait_recv()
                forward_piece(source).start()

    def arrive_panel(j):
        for p in range(pieces):
            source = j * pieces + p

            @pl.when(source % 2 != core)
            def _():
                forward_piece(source).wait_recv()

    def chain_copy(t, j, q):
        target = jnp.where(t <= zone, zone + 1, zone - 1)
        piece = solved.at[j, part(q)]
        return remote(piece, piece, s_chain.at[t, q], s_recv.at[j, q], col=target * side)

    def chain_sends(t):
        return jnp.where(t <= zone, zone < steps - 1, zone > 0)

    def side_copy(t, j, d, q):
        piece = solved.at[j, part(q)]
        return remote(piece, piece, s_side.at[t, d, q], s_recv.at[j, q], col=base + d)

    def pass_on(t, j, q):
        @pl.when(jnp.logical_and(owner, chain_sends(t)))
        def _():
            chain_copy(t, j, q).start()

        @pl.when(owner)
        def _():
            for d in range(1, side):
                side_copy(t, j, d, q).start()

    def update(j, q):
        first_row = (q - 1) * part_rows
        total = work[...]
        depth = min(2 * part_rows, cols)
        for start in range(first_row, first_row + 2 * part_rows, depth):
            total = total - dot(
                panel[j * pieces + start // cols, :, pl.ds(start % cols, depth)],
                solved[j, pl.ds(start, depth)],
            )
        work[...] = total

    per = PARTS // pieces
    my_columns = pl.ds(pl.multiple_of(chip * width, width), width)

    def row_copy(t, j, q):
        return remote(
            solved.at[j, part(q)], gathered.at[core, part(q % per), my_columns],
            s_row.at[t, q], g_recv.at[row, q % per], row=j * pieces + q // per,
        )

    def local_copy(j, q):
        return pltpu.make_async_copy(
            solved.at[j, part(q)], gathered.at[core, part(q % per), my_columns], g_local.at[q % per]
        )

    def share(t, j, q):
        @pl.when(j * pieces + q // per != row)
        def _():
            row_copy(t, j, q).start()

        @pl.when(j * pieces + q // per == row)
        def _():
            local_copy(j, q).start()

    def one_copy(m):
        return remote(send1.at[m], recv1.at[m], one_send.at[m], one_recv.at[m], row=sibling)

    def two_copy(m, d):
        return remote(send2.at[m, d - 1], recv2.at[m, d - 1], two_send.at[m, d - 1], two_recv.at[m, d - 1], row=far[d - 1])

    def first(m, carry):
        send1[m] = dot(factors_ref[span(m)], gathered[1 - core]).astype(BF16)
        one_copy(m).start()
        return carry

    def second(m, carry):
        @pl.when(m + 2 < n_swap)
        def _():
            first(m + 2, 0)

        own1[m] = dot(factors_ref[span(m)], gathered[core])
        one_copy(m).wait_recv()
        for d in range(1, chips):
            there = pl.ds(pl.multiple_of(((chip + d) % chips) * width, width), width)
            send2[m, d - 1] = (own1[m, :, there] + recv1[m, :, there].astype(F32)).astype(BF16)
            two_copy(m, d).start()
        return carry

    def third(m, carry):
        here = pl.ds(pl.multiple_of(chip * width, width), width)
        total = own1[m, :, here] + recv1[m, :, here].astype(F32)
        for d in range(1, chips):
            two_copy(m, d).wait_recv()
            total = total + recv2[m, d - 1].astype(F32)
        out_ref[span(m)] = total
        return carry

    def finish(m, carry):
        one_copy(m).wait_send()
        for d in range(1, chips):
            two_copy(m, d).wait_send()
        return carry

    n_swap = CHUNKS - n_extra

    def extra_hand_on(g, carry):
        for d in range(1, chips):
            extra_forward(g, far[d - 1]).wait_recv()
            extra_forward(g, far[d - 1]).start()
        return carry

    def extra_product(g, carry):
        rows = span(CHUNKS - 1 - g)
        total = jnp.zeros((step_rows, width), F32)
        for d in range(n_row):
            source = (row + d) % n_row
            part_of = solved[source // pieces, pl.ds(pl.multiple_of((source % pieces) * cols, cols), cols)]
            if d == 0:
                total = total + dot(factors_ref[rows], part_of)
            else:
                @pl.when(source % 2 != core)
                def _():
                    extra_forward(g, source).wait_recv()

                total = total + dot(extra[g, source], part_of)
        out_ref[rows] = total
        return carry

    def extra_finish(g, carry):
        for d in range(chips):
            extra_copy(g, d).wait_send()
        for d in range(1, chips):
            extra_forward(g, far[d - 1]).wait_send()
        return carry

    def first_products():
        factors_copy.wait()
        rhs_copy.wait()
        for q in range(per):
            local_copy(0, q).wait()
        for d in range(1, n_row):
            source = (row + d) % n_row
            for q in range(per):
                piece = gathered.at[source % 2, part(q), pl.ds(pl.multiple_of((source // 2) * width, width), width)]
                remote(piece, piece, g_local.at[q], g_recv.at[source, q], row=source).wait_recv()
        first(0, 0)
        first(1, 0)

    for t in range(steps):
        j = slot(t)
        mine = jnp.logical_and(owner, t == zone)
        if t == 0:
            hand_on(t)

        @pl.when(jnp.logical_and(owner, t != zone))
        def _():
            arrive_panel(j)

        @pl.when(mine)
        def _():
            high, low = split(work[...])
            for q in range(PARTS):
                value = work[part(q)] + solve(low_hi, low_lo, high, low, q)
                work[part(q)] = value
                solved[j, part(q)] = value.astype(BF16)
                pass_on(t, j, q)
                share(t, j, q)

        @pl.when(jnp.logical_not(mine))
        def _():
            for q in range(PARTS):
                chain_copy(t, j, q).wait_recv()
                pass_on(t, j, q)
                share(t, j, q)
                if q % 2:
                    @pl.when(owner)
                    def _():
                        update(j, q)

        hand_on(t + 1)
        if t == 0:
            lax.fori_loop(0, jnp.where(waits, n_extra, 0), extra_start, 0)

    def last_copy(q):
        target = jnp.where(zone > 0, zone - 1, 0) * side
        return remote(last.at[part(q)], solved.at[zone, part(q)], s_last.at[q], s_recv.at[zone, q], col=target)

    def solve_last():
        high, low = split(work[...])
        for q in range(PARTS):
            value = solve(up_hi, up_lo, high, low, q)
            work[part(q)] = value
            last[part(q)] = value.astype(BF16)

            @pl.when(zone > 0)
            def _():
                last_copy(q).start()

    pl.when(jnp.logical_and(owner, zone > 0))(solve_last)
    first_products()
    lax.fori_loop(0, n_swap, second, 0)
    lax.fori_loop(0, n_extra, extra_hand_on, 0)
    pl.when(jnp.logical_and(owner, zone == 0))(solve_last)
    lax.fori_loop(0, n_extra, extra_product, 0)
    lax.fori_loop(0, n_swap, third, 0)

    @pl.when(owner)
    def _():
        out_ref[pl.ds(0, block)] = rhs_ref[...] - work[...]

    lax.fori_loop(0, n_swap, finish, 0)
    lax.fori_loop(0, n_extra, extra_finish, 0)

    @pl.when(sends_panel)
    def _():
        for d in range(chips):
            panel_copy(d).wait_send()

    for t in range(steps):
        j = slot(t)

        @pl.when(jnp.logical_and(owner, t != zone))
        def _():
            for p in range(pieces):
                source = j * pieces + p

                @pl.when(jnp.logical_and(source != row, source % 2 == core))
                def _():
                    forward_piece(source).wait_send()

        @pl.when(jnp.logical_and(owner, chain_sends(t)))
        def _():
            for q in range(PARTS):
                chain_copy(t, j, q).wait_send()

        @pl.when(owner)
        def _():
            for d in range(1, side):
                for q in range(PARTS):
                    side_copy(t, j, d, q).wait_send()

        for q in range(PARTS):
            @pl.when(j * pieces + q // per != row)
            def _():
                row_copy(t, j, q).wait_send()

    @pl.when(jnp.logical_and(owner, zone > 0))
    def _():
        for q in range(PARTS):
            last_copy(q).wait_send()


def body(rhs, factors, diag_inv):
    n_row, n_col = lax.axis_size("row"), lax.axis_size("col")
    rows_dev, width = rhs.shape
    cols = factors.shape[1]
    steps, block = diag_inv.shape[:2]
    pieces, chips, side = block // cols, n_row // 2, n_col // steps
    step_rows = rows_dev // CHUNKS
    dma = pltpu.SemaphoreType.DMA
    vmem = pl.BlockSpec(memory_space=pltpu.VMEM)
    taken = pl.pallas_call(
        functools.partial(kernel, n_row, n_col, steps, block),
        out_shape=jax.ShapeDtypeStruct(rhs.shape, F32),
        in_specs=[pl.BlockSpec(memory_space=pl.ANY)] * 3,
        out_specs=vmem,
        scratch_shapes=[
            pltpu.VMEM((block, width), F32),
            pltpu.VMEM(factors.shape, BF16),
            pltpu.VMEM((GATHER, n_row, step_rows, cols), BF16),
            pltpu.VMEM((block, block), F32),
            pltpu.VMEM((block, block), BF16),
            pltpu.VMEM((block, block), BF16),
            pltpu.VMEM((block, block), BF16),
            pltpu.VMEM((block, block), BF16),
            pltpu.VMEM((n_row, block, cols), BF16),
            pltpu.VMEM((steps, block, width), BF16),
            pltpu.VMEM((block, width), BF16),
            pltpu.VMEM((block, width), F32),
            pltpu.VMEM((2, cols, chips * width), BF16),
            pltpu.VMEM((CHUNKS, step_rows, chips * width), BF16),
            pltpu.VMEM((CHUNKS, step_rows, chips * width), BF16),
            pltpu.VMEM((CHUNKS, step_rows, chips * width), F32),
            pltpu.VMEM((CHUNKS, chips - 1, step_rows, width), BF16),
            pltpu.VMEM((CHUNKS, chips - 1, step_rows, width), BF16),
            dma, dma((chips,)), dma((n_row,)), dma((chips,)),
            dma((steps, PARTS)), dma((steps, side, PARTS)), dma((steps, PARTS)), dma((steps, PARTS)), dma((PARTS,)),
            dma((PARTS // pieces,)), dma((n_row, PARTS // pieces)),
            dma((CHUNKS,)), dma((CHUNKS,)), dma((CHUNKS, chips - 1)), dma((CHUNKS, chips - 1)),
            dma((GATHER, chips)), dma((GATHER, n_row)), dma((GATHER, chips)), dma((4,)),
        ],
        compiler_params=pltpu.CompilerParams(
            collective_id=0, has_side_effects=True, vmem_limit_bytes=60 * 1024 * 1024
        ),
    )(rhs, factors, diag_inv)
    return rhs - taken


def solution(mesh):
    placed = (P("col", "row"), P("col", "row"), P())
    return jax.shard_map(
        body, mesh=mesh, in_specs=placed, out_specs=P("col", "row"), check_vma=False
    )
```

```python
import functools

import jax
import jax.numpy as jnp
from jax import lax
from jax.experimental import pallas as pl
from jax.experimental.pallas import tpu as pltpu
from jax.sharding import PartitionSpec as P

MESH = pl.DeviceIdType.MESH
F32 = jnp.float32
BF16 = jnp.bfloat16
CHUNKS = 8
PARTS = 4
GATHER = 3


def remote(src, dst, send_sem, recv_sem, **device):
    return pltpu.make_async_remote_copy(
        src_ref=src,
        dst_ref=dst,
        send_sem=send_sem,
        recv_sem=recv_sem,
        device_id=device,
        device_id_type=MESH,
    )


def dot(a, b):
    return jnp.dot(a, b, preferred_element_type=F32)


def split(value):
    high = value.astype(BF16)
    return high, (value - high.astype(F32)).astype(BF16)


def kernel(
    n_row, n_col, steps, block,
    rhs_hbm, factors_hbm, diag_ref, out_ref,
    rhs_ref, factors_ref, extra,
    diag, low_hi, low_lo, up_hi, up_lo, panel, solved, last, work, gathered,
    send1, recv1, own1, send2, recv2,
    diag_sem, f_send, f_recv, f_fwd, s_chain, s_side, s_row, s_recv, s_last, g_local, g_recv,
    one_send, one_recv, two_send, two_recv, x_send, x_recv, x_fwd, load_sem,
):
    rows_dev, width = rhs_hbm.shape
    cols = factors_ref.shape[1]
    pieces = block // cols
    chips = n_row // 2
    side = n_col // steps
    row = lax.axis_index("row")
    col = lax.axis_index("col")
    chip, core = row // 2, row % 2
    sibling = chip * 2 + 1 - core
    zone, lane = col // side, col % side
    owner = lane == 0
    base = zone * side

    diag_copy = pltpu.make_async_copy(diag_ref.at[zone], diag, diag_sem)
    rhs_copy = pltpu.make_async_copy(rhs_hbm.at[pl.ds(0, block)], rhs_ref, load_sem.at[0])
    factors_copy = pltpu.make_async_copy(factors_hbm, factors_ref, load_sem.at[1])
    work_copy = pltpu.make_async_copy(rhs_hbm.at[pl.ds(0, block)], work, load_sem.at[2])
    panel_own = pltpu.make_async_copy(factors_hbm.at[pl.ds(0, block)], panel.at[row], load_sem.at[3])
    diag_copy.start()
    work_copy.start()
    panel_own.start()
    factors_copy.start()
    rhs_copy.start()

    barrier = pltpu.get_barrier_semaphore()
    for d in range(1, n_row):
        pl.semaphore_signal(barrier, inc=1, device_id={"row": (row + d) % n_row}, device_id_type=MESH)
    for d in range(1, n_col):
        pl.semaphore_signal(barrier, inc=1, device_id={"col": (col + d) % n_col}, device_id_type=MESH)
    pl.semaphore_wait(barrier, n_row + n_col - 2)

    window = factors_hbm.at[pl.ds(0, block)]
    far = [((chip + d) % chips) * 2 + core for d in range(1, chips)]
    sends_panel = jnp.logical_and(owner, row // pieces != zone)

    def panel_copy(d):
        return remote(window, panel.at[row], f_send.at[d], f_recv.at[row], row=far[d - 1] if d else sibling)

    @pl.when(sends_panel)
    def _():
        for d in list(range(1, chips)) + [0]:
            panel_copy(d).start()

    step_rows = rows_dev // CHUNKS
    n_extra = jnp.maximum(GATHER - (zone + 1) // 2 - jnp.where(owner, 1, 0), 0)

    def span(m):
        return pl.ds(pl.multiple_of(m * step_rows, step_rows), step_rows)

    def extra_copy(g, d):
        return remote(
            factors_hbm.at[span(CHUNKS - 1 - g)], extra.at[g, row], x_send.at[g, d], x_recv.at[g, row],
            row=far[d - 1] if d else sibling,
        )

    def extra_forward(g, source):
        return remote(extra.at[g, source], extra.at[g, source], x_fwd.at[g, source // 2], x_recv.at[g, source], row=sibling)

    def extra_start(g, carry):
        for d in range(chips):
            extra_copy(g, d).start()
        return carry

    waits = jnp.logical_and(owner, zone > 0)
    lax.fori_loop(0, jnp.where(waits, 0, n_extra), extra_start, 0)
    diag_copy.wait()
    work_copy.wait()
    panel_own.wait()

    @pl.when(owner)
    def _():
        down = lax.broadcasted_iota(jnp.int32, (block, block), 0)
        across = lax.broadcasted_iota(jnp.int32, (block, block), 1)
        matrix = diag[...]
        low_hi[...], low_lo[...] = split(jnp.where(down > across, matrix, 0.0))
        up_hi[...], up_lo[...] = split(jnp.where(down <= across, matrix, 0.0))

    part_rows = block // PARTS

    def part(q):
        return pl.ds(q * part_rows, part_rows)

    def solve(hi, lo, high, low, q):
        return dot(hi[part(q)], high) + (dot(hi[part(q)], low) + dot(lo[part(q)], high))

    def forward_piece(source):
        return remote(panel.at[source], panel.at[source], f_fwd.at[source // 2], f_recv.at[source], row=sibling)

    def slot(t):
        return jnp.where(t <= zone, t, steps + zone - t)

    def hand_on(t):
        if t == steps:
            return
        for p in range(pieces):
            source = slot(t) * pieces + p
            here = jnp.logical_and(owner, t != zone)

            @pl.when(here & (source != row) & (source % 2 == core))
            def _():
                forward_piece(source).wait_recv()
                forward_piece(source).start()

    def arrive_panel(j):
        for p in range(pieces):
            source = j * pieces + p

            @pl.when(source % 2 != core)
            def _():
                forward_piece(source).wait_recv()

    def chain_copy(t, j, q):
        target = jnp.where(t <= zone, zone + 1, zone - 1)
        piece = solved.at[j, part(q)]
        return remote(piece, piece, s_chain.at[t, q], s_recv.at[j, q], col=target * side)

    def chain_sends(t):
        return jnp.where(t <= zone, zone < steps - 1, zone > 0)

    def side_copy(t, j, d, q):
        piece = solved.at[j, part(q)]
        return remote(piece, piece, s_side.at[t, d, q], s_recv.at[j, q], col=base + d)

    def pass_on(t, j, q):
        @pl.when(jnp.logical_and(owner, chain_sends(t)))
        def _():
            chain_copy(t, j, q).start()

        @pl.when(owner)
        def _():
            for d in range(1, side):
                side_copy(t, j, d, q).start()

    def update(j, q):
        first_row = (q - 1) * part_rows
        total = work[...]
        depth = min(2 * part_rows, cols)
        for start in range(first_row, first_row + 2 * part_rows, depth):
            total = total - dot(
                panel[j * pieces + start // cols, :, pl.ds(start % cols, depth)],
                solved[j, pl.ds(start, depth)],
            )
        work[...] = total

    per = PARTS // pieces
    my_columns = pl.ds(pl.multiple_of(chip * width, width), width)

    def row_copy(t, j, q):
        return remote(
            solved.at[j, part(q)], gathered.at[core, part(q % per), my_columns],
            s_row.at[t, q], g_recv.at[row, q % per], row=j * pieces + q // per,
        )

    def local_copy(j, q):
        return pltpu.make_async_copy(
            solved.at[j, part(q)], gathered.at[core, part(q % per), my_columns], g_local.at[q % per]
        )

    def share(t, j, q):
        @pl.when(j * pieces + q // per != row)
        def _():
            row_copy(t, j, q).start()

        @pl.when(j * pieces + q // per == row)
        def _():
            local_copy(j, q).start()

    def one_copy(m):
        return remote(send1.at[m], recv1.at[m], one_send.at[m], one_recv.at[m], row=sibling)

    def two_copy(m, d):
        return remote(send2.at[m, d - 1], recv2.at[m, d - 1], two_send.at[m, d - 1], two_recv.at[m, d - 1], row=far[d - 1])

    def first(m, carry):
        send1[m] = dot(factors_ref[span(m)], gathered[1 - core]).astype(BF16)
        one_copy(m).start()
        return carry

    def second(m, carry):
        @pl.when(m + 1 < n_swap)
        def _():
            first(m + 1, 0)

        own1[m] = dot(factors_ref[span(m)], gathered[core])
        one_copy(m).wait_recv()
        for d in range(1, chips):
            there = pl.ds(pl.multiple_of(((chip + d) % chips) * width, width), width)
            send2[m, d - 1] = (own1[m, :, there] + recv1[m, :, there].astype(F32)).astype(BF16)
            two_copy(m, d).start()
        return carry

    def third(m, carry):
        here = pl.ds(pl.multiple_of(chip * width, width), width)
        total = own1[m, :, here] + recv1[m, :, here].astype(F32)
        for d in range(1, chips):
            two_copy(m, d).wait_recv()
            total = total + recv2[m, d - 1].astype(F32)
        out_ref[span(m)] = total
        return carry

    def finish(m, carry):
        one_copy(m).wait_send()
        for d in range(1, chips):
            two_copy(m, d).wait_send()
        return carry

    n_swap = CHUNKS - n_extra

    def extra_hand_on(g, carry):
        for d in range(1, chips):
            extra_forward(g, far[d - 1]).wait_recv()
            extra_forward(g, far[d - 1]).start()
        return carry

    def extra_product(g, carry):
        rows = span(CHUNKS - 1 - g)
        total = jnp.zeros((step_rows, width), F32)
        for d in range(n_row):
            source = (row + d) % n_row
            part_of = solved[source // pieces, pl.ds(pl.multiple_of((source % pieces) * cols, cols), cols)]
            if d == 0:
                total = total + dot(factors_ref[rows], part_of)
            else:
                @pl.when(source % 2 != core)
                def _():
                    extra_forward(g, source).wait_recv()

                total = total + dot(extra[g, source], part_of)
        out_ref[rows] = total
        return carry

    def extra_finish(g, carry):
        for d in range(chips):
            extra_copy(g, d).wait_send()
        for d in range(1, chips):
            extra_forward(g, far[d - 1]).wait_send()
        return carry

    def first_products():
        factors_copy.wait()
        rhs_copy.wait()
        for q in range(per):
            local_copy(0, q).wait()
        for d in range(1, n_row):
            source = (row + d) % n_row
            for q in range(per):
                piece = gathered.at[source % 2, part(q), pl.ds(pl.multiple_of((source // 2) * width, width), width)]
                remote(piece, piece, g_local.at[q], g_recv.at[source, q], row=source).wait_recv()
        first(0, 0)

    for t in range(steps):
        j = slot(t)
        mine = jnp.logical_and(owner, t == zone)
        if t == 0:
            hand_on(t)

        @pl.when(jnp.logical_and(owner, t != zone))
        def _():
            arrive_panel(j)

        @pl.when(mine)
        def _():
            high, low = split(work[...])
            for q in range(PARTS):
                value = work[part(q)] + solve(low_hi, low_lo, high, low, q)
                work[part(q)] = value
                solved[j, part(q)] = value.astype(BF16)
                pass_on(t, j, q)
                share(t, j, q)

        @pl.when(jnp.logical_not(mine))
        def _():
            for q in range(PARTS):
                chain_copy(t, j, q).wait_recv()
                pass_on(t, j, q)
                share(t, j, q)
                if q % 2:
                    @pl.when(owner)
                    def _():
                        update(j, q)

        hand_on(t + 1)
        if t == 0:
            lax.fori_loop(0, jnp.where(waits, n_extra, 0), extra_start, 0)

    def last_copy(q):
        target = jnp.where(zone > 0, zone - 1, 0) * side
        return remote(last.at[part(q)], solved.at[zone, part(q)], s_last.at[q], s_recv.at[zone, q], col=target)

    def solve_last():
        high, low = split(work[...])
        for q in range(PARTS):
            value = solve(up_hi, up_lo, high, low, q)
            work[part(q)] = value
            last[part(q)] = value.astype(BF16)

            @pl.when(zone > 0)
            def _():
                last_copy(q).start()

    pl.when(jnp.logical_and(owner, zone > 0))(solve_last)
    first_products()
    lax.fori_loop(0, n_swap, second, 0)
    lax.fori_loop(0, n_extra, extra_hand_on, 0)
    pl.when(jnp.logical_and(owner, zone == 0))(solve_last)
    lax.fori_loop(0, n_extra, extra_product, 0)
    lax.fori_loop(0, n_swap, third, 0)

    @pl.when(owner)
    def _():
        out_ref[pl.ds(0, block)] = rhs_ref[...] - work[...]

    lax.fori_loop(0, n_swap, finish, 0)
    lax.fori_loop(0, n_extra, extra_finish, 0)

    @pl.when(sends_panel)
    def _():
        for d in range(chips):
            panel_copy(d).wait_send()

    for t in range(steps):
        j = slot(t)

        @pl.when(jnp.logical_and(owner, t != zone))
        def _():
            for p in range(pieces):
                source = j * pieces + p

                @pl.when(jnp.logical_and(source != row, source % 2 == core))
                def _():
                    forward_piece(source).wait_send()

        @pl.when(jnp.logical_and(owner, chain_sends(t)))
        def _():
            for q in range(PARTS):
                chain_copy(t, j, q).wait_send()

        @pl.when(owner)
        def _():
            for d in range(1, side):
                for q in range(PARTS):
                    side_copy(t, j, d, q).wait_send()

        for q in range(PARTS):
            @pl.when(j * pieces + q // per != row)
            def _():
                row_copy(t, j, q).wait_send()

    @pl.when(jnp.logical_and(owner, zone > 0))
    def _():
        for q in range(PARTS):
            last_copy(q).wait_send()


def body(rhs, factors, diag_inv):
    n_row, n_col = lax.axis_size("row"), lax.axis_size("col")
    rows_dev, width = rhs.shape
    cols = factors.shape[1]
    steps, block = diag_inv.shape[:2]
    pieces, chips, side = block // cols, n_row // 2, n_col // steps
    step_rows = rows_dev // CHUNKS
    dma = pltpu.SemaphoreType.DMA
    vmem = pl.BlockSpec(memory_space=pltpu.VMEM)
    taken = pl.pallas_call(
        functools.partial(kernel, n_row, n_col, steps, block),
        out_shape=jax.ShapeDtypeStruct(rhs.shape, F32),
        in_specs=[pl.BlockSpec(memory_space=pl.ANY)] * 3,
        out_specs=vmem,
        scratch_shapes=[
            pltpu.VMEM((block, width), F32),
            pltpu.VMEM(factors.shape, BF16),
            pltpu.VMEM((GATHER, n_row, step_rows, cols), BF16),
            pltpu.VMEM((block, block), F32),
            pltpu.VMEM((block, block), BF16),
            pltpu.VMEM((block, block), BF16),
            pltpu.VMEM((block, block), BF16),
            pltpu.VMEM((block, block), BF16),
            pltpu.VMEM((n_row, block, cols), BF16),
            pltpu.VMEM((steps, block, width), BF16),
            pltpu.VMEM((block, width), BF16),
            pltpu.VMEM((block, width), F32),
            pltpu.VMEM((2, cols, chips * width), BF16),
            pltpu.VMEM((CHUNKS, step_rows, chips * width), BF16),
            pltpu.VMEM((CHUNKS, step_rows, chips * width), BF16),
            pltpu.VMEM((CHUNKS, step_rows, chips * width), F32),
            pltpu.VMEM((CHUNKS, chips - 1, step_rows, width), BF16),
            pltpu.VMEM((CHUNKS, chips - 1, step_rows, width), BF16),
            dma, dma((chips,)), dma((n_row,)), dma((chips,)),
            dma((steps, PARTS)), dma((steps, side, PARTS)), dma((steps, PARTS)), dma((steps, PARTS)), dma((PARTS,)),
            dma((PARTS // pieces,)), dma((n_row, PARTS // pieces)),
            dma((CHUNKS,)), dma((CHUNKS,)), dma((CHUNKS, chips - 1)), dma((CHUNKS, chips - 1)),
            dma((GATHER, chips)), dma((GATHER, n_row)), dma((GATHER, chips)), dma((4,)),
        ],
        compiler_params=pltpu.CompilerParams(
            collective_id=0, has_side_effects=True, vmem_limit_bytes=60 * 1024 * 1024
        ),
    )(rhs, factors, diag_inv)
    return rhs - taken


def solution(mesh):
    placed = (P("col", "row"), P("col", "row"), P())
    return jax.shard_map(
        body, mesh=mesh, in_specs=placed, out_specs=P("col", "row"), check_vma=False
    )
```
